512 devices in a mesh: ia: 16 (over z), ja: 8 (over y, core), ka: 4 (over x).
Axes of the slice: x: 4, y: 4, z: 16, core: 2. Of those that a mesh axis runs over, the one named last changes fastest.
Arguments:
- adjoint: float32 [6, 4, 1024, 2048], P(None, 'ka', 'ja', 'ia'), may hold values from -6 to 6
- source: float32 [6, 4, 1024, 2048], P(None, 'ka', 'ja', 'ia'), may hold values from -6 to 6
- diagonal: float32 [6, 4, 1024, 2048], P(None, 'ka', 'ja', 'ia'), may hold values from 0.5 to 2
- weight_i: float32 [4, 1024, 2048], P('ka', 'ja', 'ia'), may hold values from 0.05 to 0.4
- weight_j: float32 [4, 1024, 2048], P('ka', 'ja', 'ia'), may hold values from 0.05 to 0.4
- weight_k: float32 [4, 1024, 2048], P('ka', 'ja', 'ia'), may hold values from 0.05 to 0.4
- eigvec: float32 [6, 6], replicated, may hold values from -4 to 4
- eigvec_inv: float32 [6, 6], replicated, may hold values from -4 to 4
- block_inv_i: float32 [6, 128, 128], replicated, may hold values from -1 to 2, as said below
- block_inv_j: float32 [6, 128, 128], replicated, may hold values from -1 to 2, as said below
- band_i: float32 [6, 2], replicated, may hold values from 0.25 to 0.35
- band_j: float32 [6, 2], replicated, may hold values from 0.25 to 0.35
Outputs:
- adjoint_out: float32 [6, 4, 1024, 2048], P(None, 'ka', 'ja', 'ia')
- residual: float32 [6, 4, 1024, 2048], P(None, 'ka', 'ja', 'ia')
The draws below stay inside these ranges and needn't reach their ends.
Inputs may be any that keep to these rules, and one draw needn't show every extreme that they name: `block_inv_i`: lower triangular with unit diagonal. `block_inv_j`: lower triangular with unit diagonal.
All inputs are finite; a program needn't handle non-finite values.
Results may differ from the reference program's by a relative error of at most 0.0003.
Values sent between devices are 32-bit elements; how exact they have to be, the bound alone decides.
No kernel may reach another device: no remote copies, remote signals or barrier semaphores. Data moves between devices by JAX's collectives and lax.ppermute only.
A program may use at most 64 MiB of HBM per device.

```python
import math
import jax
import jax.numpy as jnp
from jax import lax

V = 6
GROUP = 128
ITERS = 2
NI = 2048
NJ = 1024
NK = 4


def lower_blocks(key):
    rows = jnp.arange(GROUP)[:, None]
    cols = jnp.arange(GROUP)[None, :]
    noise = 0.3 * jax.random.normal(key, (V, GROUP, GROUP), jnp.float32) / jnp.sqrt(jnp.float32(GROUP))
    below = (cols < rows).astype(jnp.float32)
    strong = ((cols < 2) & (cols < rows)).astype(jnp.float32)
    unit = (cols == rows).astype(jnp.float32)
    return unit + below * noise + strong


def near_unit(key):
    mixed = 0.35 * jax.random.normal(key, (V, V), jnp.float32)
    mixed = jnp.clip(mixed, -2.5, 2.5)
    return jnp.eye(V, dtype=jnp.float32) + mixed


def draw_block_inv_i(key, part):
    return lower_blocks(jax.random.fold_in(key, 11))


def draw_block_inv_j(key, part):
    return lower_blocks(jax.random.fold_in(key, 23))


def draw_eigvec(key, part):
    return near_unit(jax.random.fold_in(key, 37))


def draw_eigvec_inv(key, part):
    return near_unit(jax.random.fold_in(key, 41))


def levels(own_key, extent, shards, smallest, largest):
    loudness, own = 1.0, jax.random.fold_in(own_key, 6)
    for dim, parts in shards:
        draws = jnp.exp(jax.random.uniform(jax.random.fold_in(own, dim), (parts,), jnp.float32, smallest / len(shards), largest / len(shards)))
        loudness = loudness * jnp.repeat(draws, extent[dim] // parts).reshape([-1 if axis == dim else 1 for axis in range(len(extent))])
    return loudness


def centred(stream_key, extent, scale, bound, split=(), kind=jnp.bfloat16):
    array = scale * jax.random.normal(stream_key, extent, jnp.float32)
    if split:
        array = array * levels(stream_key, extent, split, -0.22, 0.18)
    return jnp.clip(array, -bound, bound).astype(kind)


def setup_inputs(seed: int = 0) -> dict:
    streams_of = jax.random.split(jax.random.key(seed), 13)
    adjoint = centred(streams_of[0], (V, NK, NJ, NI), 1.0, 6.0, ((1, 4), (2, 8), (3, 16)), jnp.float32)
    source = centred(streams_of[1], (V, NK, NJ, NI), 1.0, 6.0, ((1, 4), (2, 8), (3, 16)), jnp.float32)
    diagonal = jnp.clip(0.5 + 1.5 * jax.random.uniform(streams_of[2], (V, NK, NJ, NI), jnp.float32) ** levels(streams_of[2], (V, NK, NJ, NI), ((1, 4), (2, 8), (3, 16)), -0.2, 0.2), 0.5, 2.0)
    weight_i = jnp.clip(jnp.exp(math.log(0.4) - 2.0794415 * jax.random.uniform(streams_of[3], (NK, NJ, NI), jnp.float32) ** levels(streams_of[3], (NK, NJ, NI), ((0, 4), (1, 8), (2, 16)), -0.2, 0.2)), 0.05, 0.4)
    weight_j = jnp.clip(jnp.exp(math.log(0.4) - 2.0794415 * jax.random.uniform(streams_of[4], (NK, NJ, NI), jnp.float32) ** levels(streams_of[4], (NK, NJ, NI), ((0, 4), (1, 8), (2, 16)), -0.2, 0.2)), 0.05, 0.4)
    weight_k = jnp.clip(jnp.exp(math.log(0.4) - 2.0794415 * jax.random.uniform(streams_of[5], (NK, NJ, NI), jnp.float32) ** levels(streams_of[5], (NK, NJ, NI), ((0, 4), (1, 8), (2, 16)), -0.2, 0.2)), 0.05, 0.4)
    eigvec = draw_eigvec(jax.random.fold_in(streams_of[12], 71), 0)
    eigvec_inv = draw_eigvec_inv(jax.random.fold_in(streams_of[12], 71), 0)
    block_inv_i = draw_block_inv_i(jax.random.fold_in(streams_of[12], 71), 0)
    block_inv_j = draw_block_inv_j(jax.random.fold_in(streams_of[12], 71), 0)
    band_i = jnp.clip(jax.random.uniform(streams_of[10], (V, 2), jnp.float32, 0.25, 0.35), 0.25, 0.35)
    band_j = jnp.clip(jax.random.uniform(streams_of[11], (V, 2), jnp.float32, 0.25, 0.35), 0.25, 0.35)
    return {"adjoint": adjoint, "source": source, "diagonal": diagonal, "weight_i": weight_i, "weight_j": weight_j, "weight_k": weight_k, "eigvec": eigvec, "eigvec_inv": eigvec_inv, "block_inv_i": block_inv_i, "block_inv_j": block_inv_j, "band_i": band_i, "band_j": band_j}


def solve_block(piece, dinv, band, first_prev, last_prev):
    shape = (-1,) + (1,) * (piece.ndim - 2)
    coef_one = band[:, 0].reshape(shape)
    coef_two = band[:, 1].reshape(shape)
    head = piece[..., 0] - (coef_one * last_prev + coef_two * first_prev)
    second = piece[..., 1] - coef_two * last_prev
    rhs_block = jnp.concatenate([head[..., None], second[..., None], piece[..., 2:]], axis=-1)
    return jnp.einsum('vabm,vnm->vabn', rhs_block, dinv, precision=lax.Precision.HIGHEST)


def line_solve(field, dinv, band):
    nvar, dim_a, dim_b, length = field.shape
    width = dinv.shape[-1]
    pieces = jnp.moveaxis(field.reshape(nvar, dim_a, dim_b, length // width, width), 3, 0)

    def advance(carry, piece):
        out = solve_block(piece, dinv, band, carry[0], carry[1])
        return (out[..., width - 2], out[..., width - 1]), out

    zeros = jnp.zeros((nvar, dim_a, dim_b), jnp.float32)
    _, outs = lax.scan(advance, (zeros, zeros), pieces)
    return jnp.moveaxis(outs, 0, 3).reshape(nvar, dim_a, dim_b, length)


def explicit_residual(state, source, diagonal, weight_i, weight_j, weight_k):
    padded = jnp.pad(state, ((0, 0), (1, 1), (1, 1), (1, 1)))
    near_i = padded[:, 1:-1, 1:-1, 2:] + padded[:, 1:-1, 1:-1, :-2]
    near_j = padded[:, 1:-1, 2:, 1:-1] + padded[:, 1:-1, :-2, 1:-1]
    near_k = padded[:, 2:, 1:-1, 1:-1] + padded[:, :-2, 1:-1, 1:-1]
    return source - diagonal * state + weight_i[None] * near_i + weight_j[None] * near_j + weight_k[None] * near_k


def reference(adjoint, source, diagonal, weight_i, weight_j, weight_k, eigvec, eigvec_inv, block_inv_i, block_inv_j, band_i, band_j):
    state = adjoint
    residual = source
    for step in range(ITERS):
        residual = explicit_residual(state, source, diagonal, weight_i, weight_j, weight_k)
        chars = jnp.einsum('uv,vkji->ukji', eigvec_inv, residual, precision=lax.Precision.HIGHEST)
        chars = line_solve(chars, block_inv_i, band_i)
        turned = jnp.swapaxes(chars, 2, 3)
        turned = line_solve(turned, block_inv_j, band_j)
        chars = jnp.swapaxes(turned, 2, 3)
        state = state + jnp.einsum('uv,vkji->ukji', eigvec, chars, precision=lax.Precision.HIGHEST)
    return state, residual
```

```python
import jax
import jax.numpy as jnp
from jax import lax
from jax.sharding import PartitionSpec as P

ITERS = 2
HI = lax.Precision.HIGHEST


def shifted(value, axis, by):
    length = lax.axis_size(axis)
    pairs = [(i, i + by) for i in range(length) if 0 <= i + by < length]
    return lax.ppermute(value, axis, pairs)


def inflow_terms(dinv, band):
    coef_one = band[:, 0][:, None]
    coef_two = band[:, 1][:, None]
    resp_last = -(coef_one * dinv[:, :, 0] + coef_two * dinv[:, :, 1])
    resp_first = -coef_two * dinv[:, :, 0]
    return resp_first, resp_last


def carry_powers(resp_first, resp_last, count):
    width = resp_first.shape[-1]
    top = jnp.stack([resp_first[:, width - 2], resp_last[:, width - 2]], axis=-1)
    bottom = jnp.stack([resp_first[:, width - 1], resp_last[:, width - 1]], axis=-1)
    step = jnp.stack([top, bottom], axis=-2)
    eye = jnp.broadcast_to(jnp.eye(2, dtype=step.dtype), step.shape)
    powers = eye[None]
    lead = step
    while powers.shape[0] < count:
        more = jnp.einsum("kvab,vbc->kvac", powers, lead, precision=HI)
        powers = jnp.concatenate([powers, more], axis=0)
        lead = jnp.einsum("vab,vbc->vac", more[-1], step, precision=HI)
    return powers[:count]


def inbound_ends(ends, powers, axis):
    count = lax.axis_size(axis)
    me = lax.axis_index(axis)
    gathered = lax.all_gather(ends, axis)
    lag = me - 1 - jnp.arange(count)
    table = jnp.take(powers, jnp.clip(lag, 0, count - 1), axis=0)
    table = jnp.where((lag >= 0)[:, None, None, None], table, 0.0)
    return jnp.einsum("cvad,cdvn->avn", table, gathered, precision=HI)


def local(
    adjoint,
    source,
    diagonal,
    weight_i,
    weight_j,
    weight_k,
    eigvec,
    eigvec_inv,
    block_inv_i,
    block_inv_j,
    band_i,
    band_j,
):
    nv = adjoint.shape[0]
    nj, ni = adjoint.shape[2], adjoint.shape[3]
    width = block_inv_i.shape[-1]
    state = adjoint.reshape(nv, nj, ni)
    src = source.reshape(nv, nj, ni)
    diag = diagonal.reshape(nv, nj, ni)
    wi = weight_i.reshape(1, nj, ni)
    wj = weight_j.reshape(1, nj, ni)
    wk = weight_k.reshape(1, nj, ni)

    first_i, last_i = inflow_terms(block_inv_i, band_i)
    first_j, last_j = inflow_terms(block_inv_j, band_j)
    pow_i = carry_powers(first_i, last_i, lax.axis_size("ia"))
    pow_j = carry_powers(first_j, last_j, lax.axis_size("ja"))

    residual = src
    for step in range(ITERS):
        lo_i = shifted(state[:, :, ni - 1], "ia", 1)
        hi_i = shifted(state[:, :, 0], "ia", -1)
        lo_j = shifted(state[:, nj - 1, :], "ja", 1)
        hi_j = shifted(state[:, 0, :], "ja", -1)
        lo_k = shifted(state, "ka", 1)
        hi_k = shifted(state, "ka", -1)
        right_i = jnp.concatenate([state[:, :, 1:], hi_i[:, :, None]], axis=2)
        left_i = jnp.concatenate([lo_i[:, :, None], state[:, :, :-1]], axis=2)
        up_j = jnp.concatenate([state[:, 1:, :], hi_j[:, None, :]], axis=1)
        down_j = jnp.concatenate([lo_j[:, None, :], state[:, :-1, :]], axis=1)
        residual = (
            src
            - diag * state
            + wi * (right_i + left_i)
            + wj * (up_j + down_j)
            + wk * (hi_k + lo_k)
        )
        chars = jnp.einsum("uv,vji->uji", eigvec_inv, residual, precision=HI)
        plain_i = jnp.einsum("vjm,vnm->vjn", chars, block_inv_i, precision=HI)
        ends_i = jnp.stack([plain_i[:, :, width - 2], plain_i[:, :, width - 1]])
        in_i = inbound_ends(ends_i, pow_i, "ia")
        chars = (
            plain_i
            + in_i[0][:, :, None] * first_i[:, None, :]
            + in_i[1][:, :, None] * last_i[:, None, :]
        )
        plain_j = jnp.einsum("vnm,vmi->vni", block_inv_j, chars, precision=HI)
        ends_j = jnp.stack([plain_j[:, width - 2, :], plain_j[:, width - 1, :]])
        in_j = inbound_ends(ends_j, pow_j, "ja")
        chars = (
            plain_j
            + in_j[0][:, None, :] * first_j[:, :, None]
            + in_j[1][:, None, :] * last_j[:, :, None]
        )
        state = state + jnp.einsum("uv,vji->uji", eigvec, chars, precision=HI)
    return (state.reshape(adjoint.shape), residual.reshape(adjoint.shape))


def solution(mesh):
    return jax.shard_map(
        local,
        mesh=mesh,
        in_specs=(
            P(None, "ka", "ja", "ia"),
            P(None, "ka", "ja", "ia"),
            P(None, "ka", "ja", "ia"),
            P("ka", "ja", "ia"),
            P("ka", "ja", "ia"),
            P("ka", "ja", "ia"),
            P(),
            P(),
            P(),
            P(),
            P(),
            P(),
        ),
        out_specs=(P(None, "ka", "ja", "ia"), P(None, "ka", "ja", "ia")),
        check_vma=False,
    )
```

```python
import jax
import jax.numpy as jnp
from jax import lax
from jax.sharding import PartitionSpec as P

ITERS = 2
HI = lax.Precision.HIGHEST


def shifted(value, axis, by):
    length = lax.axis_size(axis)
    pairs = [(i, i + by) for i in range(length) if 0 <= i + by < length]
    return lax.ppermute(value, axis, pairs)


def inflow_terms(dinv, band):
    coef_one = band[:, 0][:, None]
    coef_two = band[:, 1][:, None]
    resp_last = -(coef_one * dinv[:, :, 0] + coef_two * dinv[:, :, 1])
    resp_first = -coef_two * dinv[:, :, 0]
    return resp_first, resp_last


def carry_powers(resp_first, resp_last, count):
    width = resp_first.shape[-1]
    top = jnp.stack([resp_first[:, width - 2], resp_last[:, width - 2]], axis=-1)
    bottom = jnp.stack([resp_first[:, width - 1], resp_last[:, width - 1]], axis=-1)
    step = jnp.stack([top, bottom], axis=-2)
    eye = jnp.broadcast_to(jnp.eye(2, dtype=step.dtype), step.shape)
    powers = eye[None]
    lead = step
    while powers.shape[0] < count:
        more = jnp.einsum("kvab,vbc->kvac", powers, lead, precision=HI)
        powers = jnp.concatenate([powers, more], axis=0)
        lead = jnp.einsum("vab,vbc->vac", more[-1], step, precision=HI)
    return powers[:count]


def inbound_ends(ends, powers, axis):
    count = lax.axis_size(axis)
    total = ends
    inbound = None
    dist = 1
    while dist < count:
        recv = shifted(total, axis, dist)
        if inbound is None:
            inbound = recv
        else:
            inbound = inbound + jnp.einsum("vad,dvn->avn", powers[dist - 1], recv, precision=HI)
        if 2 * dist < count:
            total = total + jnp.einsum("vad,dvn->avn", powers[dist], recv, precision=HI)
        dist *= 2
    return inbound


def local(
    adjoint,
    source,
    diagonal,
    weight_i,
    weight_j,
    weight_k,
    eigvec,
    eigvec_inv,
    block_inv_i,
    block_inv_j,
    band_i,
    band_j,
):
    nv = adjoint.shape[0]
    nj, ni = adjoint.shape[2], adjoint.shape[3]
    width = block_inv_i.shape[-1]
    state = adjoint.reshape(nv, nj, ni)
    src = source.reshape(nv, nj, ni)
    diag = diagonal.reshape(nv, nj, ni)
    wi = weight_i.reshape(1, nj, ni)
    wj = weight_j.reshape(1, nj, ni)
    wk = weight_k.reshape(1, nj, ni)

    first_i, last_i = inflow_terms(block_inv_i, band_i)
    first_j, last_j = inflow_terms(block_inv_j, band_j)
    pow_i = carry_powers(first_i, last_i, lax.axis_size("ia") // 2 + 1)
    pow_j = carry_powers(first_j, last_j, lax.axis_size("ja") // 2 + 1)

    residual = src
    for step in range(ITERS):
        lo_i = shifted(state[:, :, ni - 1], "ia", 1)
        hi_i = shifted(state[:, :, 0], "ia", -1)
        lo_j = shifted(state[:, nj - 1, :], "ja", 1)
        hi_j = shifted(state[:, 0, :], "ja", -1)
        lo_k = shifted(state, "ka", 1)
        hi_k = shifted(state, "ka", -1)
        right_i = jnp.concatenate([state[:, :, 1:], hi_i[:, :, None]], axis=2)
        left_i = jnp.concatenate([lo_i[:, :, None], state[:, :, :-1]], axis=2)
        up_j = jnp.concatenate([state[:, 1:, :], hi_j[:, None, :]], axis=1)
        down_j = jnp.concatenate([lo_j[:, None, :], state[:, :-1, :]], axis=1)
        residual = (
            src
            - diag * state
            + wi * (right_i + left_i)
            + wj * (up_j + down_j)
            + wk * (hi_k + lo_k)
        )
        chars = jnp.einsum("uv,vji->uji", eigvec_inv, residual, precision=HI)
        plain_i = jnp.einsum("vjm,vnm->vjn", chars, block_inv_i, precision=HI)
        ends_i = jnp.stack([plain_i[:, :, width - 2], plain_i[:, :, width - 1]])
        in_i = inbound_ends(ends_i, pow_i, "ia")
        chars = (
            plain_i
            + in_i[0][:, :, None] * first_i[:, None, :]
            + in_i[1][:, :, None] * last_i[:, None, :]
        )
        plain_j = jnp.einsum("vnm,vmi->vni", block_inv_j, chars, precision=HI)
        ends_j = jnp.stack([plain_j[:, width - 2, :], plain_j[:, width - 1, :]])
        in_j = inbound_ends(ends_j, pow_j, "ja")
        chars = (
            plain_j
            + in_j[0][:, None, :] * first_j[:, :, None]
            + in_j[1][:, None, :] * last_j[:, :, None]
        )
        state = state + jnp.einsum("uv,vji->uji", eigvec, chars, precision=HI)
    return (state.reshape(adjoint.shape), residual.reshape(adjoint.shape))


def solution(mesh):
    return jax.shard_map(
        local,
        mesh=mesh,
        in_specs=(
            P(None, "ka", "ja", "ia"),
            P(None, "ka", "ja", "ia"),
            P(None, "ka", "ja", "ia"),
            P("ka", "ja", "ia"),
            P("ka", "ja", "ia"),
            P("ka", "ja", "ia"),
            P(),
            P(),
            P(),
            P(),
            P(),
            P(),
        ),
        out_specs=(P(None, "ka", "ja", "ia"), P(None, "ka", "ja", "ia")),
        check_vma=False,
    )
```

```python
import jax
import jax.numpy as jnp
from jax import lax
from jax.sharding import PartitionSpec as P

ITERS = 2
HI = lax.Precision.HIGHEST


def shifted(value, axis, by):
    length = lax.axis_size(axis)
    pairs = [(i, i + by) for i in range(length) if 0 <= i + by < length]
    return lax.ppermute(value, axis, pairs)


def inflow_terms(dinv, band):
    coef_one = band[:, 0][:, None]
    coef_two = band[:, 1][:, None]
    resp_last = -(coef_one * dinv[:, :, 0] + coef_two * dinv[:, :, 1])
    resp_first = -coef_two * dinv[:, :, 0]
    return resp_first, resp_last


def carry_powers(resp_first, resp_last, count):
    width = resp_first.shape[-1]
    top = jnp.stack([resp_first[:, width - 2], resp_last[:, width - 2]], axis=-1)
    bottom = jnp.stack([resp_first[:, width - 1], resp_last[:, width - 1]], axis=-1)
    step = jnp.stack([top, bottom], axis=-2)
    eye = jnp.broadcast_to(jnp.eye(2, dtype=step.dtype), step.shape)
    powers = eye[None]
    lead = step
    while powers.shape[0] < count:
        more = jnp.einsum("kvab,vbc->kvac", powers, lead, precision=HI)
        powers = jnp.concatenate([powers, more], axis=0)
        lead = jnp.einsum("vab,vbc->vac", more[-1], step, precision=HI)
    return powers[:count]


def inbound_ends(ends, powers, axis):
    count = lax.axis_size(axis)
    me = lax.axis_index(axis)
    lag = jnp.arange(count) - 1 - me
    table = jnp.take(powers, jnp.clip(lag, 0, count - 1), axis=0)
    table = jnp.where((lag >= 0)[:, None, None, None], table, 0.0)
    spread = jnp.einsum("bvad,dvn->bavn", table, ends, precision=HI)
    return lax.psum_scatter(spread, axis, scatter_dimension=0, tiled=False)


def local(
    adjoint,
    source,
    diagonal,
    weight_i,
    weight_j,
    weight_k,
    eigvec,
    eigvec_inv,
    block_inv_i,
    block_inv_j,
    band_i,
    band_j,
):
    nv = adjoint.shape[0]
    nj, ni = adjoint.shape[2], adjoint.shape[3]
    width = block_inv_i.shape[-1]
    state = adjoint.reshape(nv, nj, ni)
    src = source.reshape(nv, nj, ni)
    diag = diagonal.reshape(nv, nj, ni)
    wi = weight_i.reshape(1, nj, ni)
    wj = weight_j.reshape(1, nj, ni)
    wk = weight_k.reshape(1, nj, ni)

    first_i, last_i = inflow_terms(block_inv_i, band_i)
    first_j, last_j = inflow_terms(block_inv_j, band_j)
    pow_i = carry_powers(first_i, last_i, lax.axis_size("ia"))
    pow_j = carry_powers(first_j, last_j, lax.axis_size("ja"))

    residual = src
    for step in range(ITERS):
        lo_i = shifted(state[:, :, ni - 1], "ia", 1)
        hi_i = shifted(state[:, :, 0], "ia", -1)
        lo_j = shifted(state[:, nj - 1, :], "ja", 1)
        hi_j = shifted(state[:, 0, :], "ja", -1)
        lo_k = shifted(state, "ka", 1)
        hi_k = shifted(state, "ka", -1)
        right_i = jnp.concatenate([state[:, :, 1:], hi_i[:, :, None]], axis=2)
        left_i = jnp.concatenate([lo_i[:, :, None], state[:, :, :-1]], axis=2)
        up_j = jnp.concatenate([state[:, 1:, :], hi_j[:, None, :]], axis=1)
        down_j = jnp.concatenate([lo_j[:, None, :], state[:, :-1, :]], axis=1)
        residual = (
            src
            - diag * state
            + wi * (right_i + left_i)
            + wj * (up_j + down_j)
            + wk * (hi_k + lo_k)
        )
        chars = jnp.einsum("uv,vji->uji", eigvec_inv, residual, precision=HI)
        plain_i = jnp.einsum("vjm,vnm->vjn", chars, block_inv_i, precision=HI)
        ends_i = jnp.stack([plain_i[:, :, width - 2], plain_i[:, :, width - 1]])
        in_i = inbound_ends(ends_i, pow_i, "ia")
        chars = (
            plain_i
            + in_i[0][:, :, None] * first_i[:, None, :]
            + in_i[1][:, :, None] * last_i[:, None, :]
        )
        plain_j = jnp.einsum("vnm,vmi->vni", block_inv_j, chars, precision=HI)
        ends_j = jnp.stack([plain_j[:, width - 2, :], plain_j[:, width - 1, :]])
        in_j = inbound_ends(ends_j, pow_j, "ja")
        chars = (
            plain_j
            + in_j[0][:, None, :] * first_j[:, :, None]
            + in_j[1][:, None, :] * last_j[:, :, None]
        )
        state = state + jnp.einsum("uv,vji->uji", eigvec, chars, precision=HI)
    return (state.reshape(adjoint.shape), residual.reshape(adjoint.shape))


def solution(mesh):
    return jax.shard_map(
        local,
        mesh=mesh,
        in_specs=(
            P(None, "ka", "ja", "ia"),
            P(None, "ka", "ja", "ia"),
            P(None, "ka", "ja", "ia"),
            P("ka", "ja", "ia"),
            P("ka", "ja", "ia"),
            P("ka", "ja", "ia"),
            P(),
            P(),
            P(),
            P(),
            P(),
            P(),
        ),
        out_specs=(P(None, "ka", "ja", "ia"), P(None, "ka", "ja", "ia")),
        check_vma=False,
    )
```

```python
import jax
import jax.numpy as jnp
from jax import lax
from jax.experimental import pallas as pl
from jax.experimental.pallas import tpu as pltpu
from jax.sharding import PartitionSpec as P

ITERS = 2
HI = lax.Precision.HIGHEST


def shifted(value, axis, by):
    length = lax.axis_size(axis)
    pairs = [(i, i + by) for i in range(length) if 0 <= i + by < length]
    return lax.ppermute(value, axis, pairs)


def inflow_terms(dinv, band):
    coef_one = band[:, 0][:, None]
    coef_two = band[:, 1][:, None]
    resp_last = -(coef_one * dinv[:, :, 0] + coef_two * dinv[:, :, 1])
    resp_first = -coef_two * dinv[:, :, 0]
    return resp_first, resp_last


def carry_powers(resp_first, resp_last, count):
    width = resp_first.shape[-1]
    top = jnp.stack([resp_first[:, width - 2], resp_last[:, width - 2]], axis=-1)
    bottom = jnp.stack([resp_first[:, width - 1], resp_last[:, width - 1]], axis=-1)
    step = jnp.stack([top, bottom], axis=-2)
    eye = jnp.broadcast_to(jnp.eye(2, dtype=step.dtype), step.shape)
    powers = eye[None]
    lead = step
    while powers.shape[0] < count:
        more = jnp.einsum("kvab,vbc->kvac", powers, lead, precision=HI)
        powers = jnp.concatenate([powers, more], axis=0)
        lead = jnp.einsum("vab,vbc->vac", more[-1], step, precision=HI)
    return powers[:count]


def inbound_ends(ends, powers, axis):
    count = lax.axis_size(axis)
    me = lax.axis_index(axis)
    gathered = lax.all_gather(ends, axis)
    lag = me - 1 - jnp.arange(count)
    table = jnp.take(powers, jnp.clip(lag, 0, count - 1), axis=0)
    table = jnp.where((lag >= 0)[:, None, None, None], table, 0.0)
    return jnp.einsum("cvad,cdvn->avn", table, gathered, precision=HI)


def _vmem():
    return pl.BlockSpec(memory_space=pltpu.VMEM)


def _smem():
    return pl.BlockSpec(memory_space=pltpu.SMEM)


def _mm(a, b):
    return jnp.dot(a, b, precision=HI, preferred_element_type=jnp.float32)


def residual_kernel(state, src, diag, wi, wj, wk, lo_i, hi_i, lo_j, hi_j, lo_k, hi_k, mix, dinv_t,
                    res_out, plain_out, chars):
    nv, nj, ni = state.shape
    lane = lax.broadcasted_iota(jnp.int32, (nj, ni), 1)
    row = lax.broadcasted_iota(jnp.int32, (nj, ni), 0)
    for v in range(nv):
        x = state[v]
        right_i = jnp.where(lane == ni - 1, hi_i[v], pltpu.roll(x, ni - 1, 1))
        left_i = jnp.where(lane == 0, lo_i[v], pltpu.roll(x, 1, 1))
        up_j = jnp.where(row == nj - 1, hi_j[v], pltpu.roll(x, nj - 1, 0))
        down_j = jnp.where(row == 0, lo_j[v], pltpu.roll(x, 1, 0))
        res_out[v] = (
            src[v]
            - diag[v] * x
            + wi[...] * (right_i + left_i)
            + wj[...] * (up_j + down_j)
            + wk[...] * (hi_k[v] + lo_k[v])
        )
    for u in range(nv):
        acc = mix[u, 0] * res_out[0]
        for v in range(1, nv):
            acc = acc + mix[u, v] * res_out[v]
        chars[u] = acc
    for u in range(nv):
        plain_out[u] = _mm(chars[u], dinv_t[u])


def across_i_kernel(plain, in_first, in_last, first, last, dinv, out):
    nv = plain.shape[0]
    for v in range(nv):
        fixed = plain[v] + in_first[v] * first[v] + in_last[v] * last[v]
        out[v] = _mm(dinv[v], fixed)


def update_kernel(state, plain, in_first, in_last, first, last, mix, out, chars):
    nv = plain.shape[0]
    for v in range(nv):
        chars[v] = plain[v] + in_first[v] * first[v] + in_last[v] * last[v]
    for u in range(nv):
        acc = state[u]
        total = mix[u, 0] * chars[0]
        for v in range(1, nv):
            total = total + mix[u, v] * chars[v]
        out[u] = acc + total


def _call(kernel, n_in, smem_at, outs, scratch):
    specs = [_smem() if k in smem_at else _vmem() for k in range(n_in)]
    return pl.pallas_call(
        kernel,
        out_shape=outs,
        in_specs=specs,
        out_specs=tuple(_vmem() for _ in outs) if isinstance(outs, tuple) else _vmem(),
        scratch_shapes=scratch,
    )


def local(
    adjoint,
    source,
    diagonal,
    weight_i,
    weight_j,
    weight_k,
    eigvec,
    eigvec_inv,
    block_inv_i,
    block_inv_j,
    band_i,
    band_j,
):
    nv = adjoint.shape[0]
    nj, ni = adjoint.shape[2], adjoint.shape[3]
    width = block_inv_i.shape[-1]
    state = adjoint.reshape(nv, nj, ni)
    src = source.reshape(nv, nj, ni)
    diag = diagonal.reshape(nv, nj, ni)
    wi = weight_i.reshape(1, nj, ni)
    wj = weight_j.reshape(1, nj, ni)
    wk = weight_k.reshape(1, nj, ni)

    first_i, last_i = inflow_terms(block_inv_i, band_i)
    first_j, last_j = inflow_terms(block_inv_j, band_j)
    pow_i = carry_powers(first_i, last_i, lax.axis_size("ia"))
    pow_j = carry_powers(first_j, last_j, lax.axis_size("ja"))

    blk = jax.ShapeDtypeStruct((nv, nj, ni), jnp.float32)
    res_call = _call(residual_kernel, 14, (12,), (blk, blk), [pltpu.VMEM((nv, nj, ni), jnp.float32)])
    across_call = _call(across_i_kernel, 6, (), blk, [])
    update_call = _call(update_kernel, 7, (6,), blk, [pltpu.VMEM((nv, nj, ni), jnp.float32)])
    dinv_i_t = jnp.swapaxes(block_inv_i, 1, 2)
    first_i_row, last_i_row = first_i[:, None, :], last_i[:, None, :]
    first_j_col, last_j_col = first_j[:, :, None], last_j[:, :, None]

    residual = src
    for step in range(ITERS):
        lo_i = shifted(state[:, :, ni - 1 :], "ia", 1)
        hi_i = shifted(state[:, :, :1], "ia", -1)
        lo_j = shifted(state[:, nj - 1 :, :], "ja", 1)
        hi_j = shifted(state[:, :1, :], "ja", -1)
        lo_k = shifted(state, "ka", 1)
        hi_k = shifted(state, "ka", -1)
        residual, plain_i = res_call(
            state, src, diag, wi[0], wj[0], wk[0], lo_i, hi_i, lo_j, hi_j, lo_k, hi_k, eigvec_inv, dinv_i_t
        )
        ends_i = jnp.stack([plain_i[:, :, width - 2], plain_i[:, :, width - 1]])
        in_i = inbound_ends(ends_i, pow_i, "ia")
        plain_j = across_call(
            plain_i, in_i[0][:, :, None], in_i[1][:, :, None], first_i_row, last_i_row, block_inv_j
        )
        ends_j = jnp.stack([plain_j[:, width - 2, :], plain_j[:, width - 1, :]])
        in_j = inbound_ends(ends_j, pow_j, "ja")
        state = update_call(
            state, plain_j, in_j[0][:, None, :], in_j[1][:, None, :], first_j_col, last_j_col, eigvec
        )
    return (state.reshape(adjoint.shape), residual.reshape(adjoint.shape))


def solution(mesh):
    return jax.shard_map(
        local,
        mesh=mesh,
        in_specs=(
            P(None, "ka", "ja", "ia"),
            P(None, "ka", "ja", "ia"),
            P(None, "ka", "ja", "ia"),
            P("ka", "ja", "ia"),
            P("ka", "ja", "ia"),
            P("ka", "ja", "ia"),
            P(),
            P(),
            P(),
            P(),
            P(),
            P(),
        ),
        out_specs=(P(None, "ka", "ja", "ia"), P(None, "ka", "ja", "ia")),
        check_vma=False,
    )
```

```python
import jax
import jax.numpy as jnp
from jax import lax
from jax.experimental import pallas as pl
from jax.experimental.pallas import tpu as pltpu
from jax.sharding import PartitionSpec as P

ITERS = 2
HI = lax.Precision.HIGHEST


def shifted(value, axis, by):
    length = lax.axis_size(axis)
    pairs = [(i, i + by) for i in range(length) if 0 <= i + by < length]
    return lax.ppermute(value, axis, pairs)


def inflow_terms(dinv, band):
    coef_one = band[:, 0][:, None]
    coef_two = band[:, 1][:, None]
    resp_last = -(coef_one * dinv[:, :, 0] + coef_two * dinv[:, :, 1])
    resp_first = -coef_two * dinv[:, :, 0]
    return resp_first, resp_last


def carry_powers(resp_first, resp_last, count):
    width = resp_first.shape[-1]
    top = jnp.stack([resp_first[:, width - 2], resp_last[:, width - 2]], axis=-1)
    bottom = jnp.stack([resp_first[:, width - 1], resp_last[:, width - 1]], axis=-1)
    step = jnp.stack([top, bottom], axis=-2)
    eye = jnp.broadcast_to(jnp.eye(2, dtype=step.dtype), step.shape)
    powers = eye[None]
    lead = step
    while powers.shape[0] < count:
        more = jnp.einsum("kvab,vbc->kvac", powers, lead, precision=HI)
        powers = jnp.concatenate([powers, more], axis=0)
        lead = jnp.einsum("vab,vbc->vac", more[-1], step, precision=HI)
    return powers[:count]


def inbound_ends(ends, powers, axis):
    count = lax.axis_size(axis)
    me = lax.axis_index(axis)
    gathered = lax.all_gather(ends, axis)
    lag = me - 1 - jnp.arange(count)
    table = jnp.take(powers, jnp.clip(lag, 0, count - 1), axis=0)
    table = jnp.where((lag >= 0)[:, None, None, None], table, 0.0)
    return jnp.einsum("cvad,cdvn->avn", table, gathered, precision=HI)


def _vmem():
    return pl.BlockSpec(memory_space=pltpu.VMEM)


def _smem():
    return pl.BlockSpec(memory_space=pltpu.SMEM)


def _mm(a, b):
    return jnp.dot(a, b, precision=HI, preferred_element_type=jnp.float32)


def _column(vec, shape):
    return jnp.transpose(jnp.broadcast_to(vec, (shape[1], shape[0])))


def residual_kernel(state, src, diag, wi, wj, wk, lo_i, hi_i, lo_j, hi_j, lo_k, hi_k, mix, dinv_t,
                    res_out, plain_out, chars):
    nv, nj, ni = state.shape
    lane = lax.broadcasted_iota(jnp.int32, (nj, ni), 1)
    row = lax.broadcasted_iota(jnp.int32, (nj, ni), 0)
    for v in range(nv):
        x = state[v]
        right_i = jnp.where(lane == ni - 1, _column(hi_i[v], (nj, ni)), pltpu.roll(x, ni - 1, 1))
        left_i = jnp.where(lane == 0, _column(lo_i[v], (nj, ni)), pltpu.roll(x, 1, 1))
        up_j = jnp.where(row == nj - 1, hi_j[v], pltpu.roll(x, nj - 1, 0))
        down_j = jnp.where(row == 0, lo_j[v], pltpu.roll(x, 1, 0))
        res_out[v] = (
            src[v]
            - diag[v] * x
            + wi[...] * (right_i + left_i)
            + wj[...] * (up_j + down_j)
            + wk[...] * (hi_k[v] + lo_k[v])
        )
    for u in range(nv):
        acc = mix[u, 0] * res_out[0]
        for v in range(1, nv):
            acc = acc + mix[u, v] * res_out[v]
        chars[u] = acc
    for u in range(nv):
        plain_out[u] = _mm(chars[u], dinv_t[u])


def across_i_kernel(plain, in_first, in_last, first, last, dinv, out):
    nv = plain.shape[0]
    shape = plain.shape[1:]
    for v in range(nv):
        fixed = (
            plain[v]
            + _column(in_first[v], shape) * first[v]
            + _column(in_last[v], shape) * last[v]
        )
        out[v] = _mm(dinv[v], fixed)


def update_kernel(state, plain, in_first, in_last, first, last, mix, out, chars):
    nv = plain.shape[0]
    for v in range(nv):
        chars[v] = plain[v] + in_first[v] * first[v] + in_last[v] * last[v]
    for u in range(nv):
        acc = state[u]
        total = mix[u, 0] * chars[0]
        for v in range(1, nv):
            total = total + mix[u, v] * chars[v]
        out[u] = acc + total


def _call(kernel, n_in, smem_at, outs, scratch):
    specs = [_smem() if k in smem_at else _vmem() for k in range(n_in)]
    return pl.pallas_call(
        kernel,
        out_shape=outs,
        in_specs=specs,
        out_specs=tuple(_vmem() for _ in outs) if isinstance(outs, tuple) else _vmem(),
        scratch_shapes=scratch,
    )


def local(
    adjoint,
    source,
    diagonal,
    weight_i,
    weight_j,
    weight_k,
    eigvec,
    eigvec_inv,
    block_inv_i,
    block_inv_j,
    band_i,
    band_j,
):
    nv = adjoint.shape[0]
    nj, ni = adjoint.shape[2], adjoint.shape[3]
    width = block_inv_i.shape[-1]
    state = adjoint.reshape(nv, nj, ni)
    src = source.reshape(nv, nj, ni)
    diag = diagonal.reshape(nv, nj, ni)
    wi = weight_i.reshape(1, nj, ni)
    wj = weight_j.reshape(1, nj, ni)
    wk = weight_k.reshape(1, nj, ni)

    first_i, last_i = inflow_terms(block_inv_i, band_i)
    first_j, last_j = inflow_terms(block_inv_j, band_j)
    pow_i = carry_powers(first_i, last_i, lax.axis_size("ia"))
    pow_j = carry_powers(first_j, last_j, lax.axis_size("ja"))

    blk = jax.ShapeDtypeStruct((nv, nj, ni), jnp.float32)
    res_call = _call(residual_kernel, 14, (12,), (blk, blk), [pltpu.VMEM((nv, nj, ni), jnp.float32)])
    across_call = _call(across_i_kernel, 6, (), blk, [])
    update_call = _call(update_kernel, 7, (6,), blk, [pltpu.VMEM((nv, nj, ni), jnp.float32)])
    dinv_i_t = jnp.swapaxes(block_inv_i, 1, 2)
    first_i_row, last_i_row = first_i[:, None, :], last_i[:, None, :]
    first_j_col, last_j_col = first_j[:, :, None], last_j[:, :, None]

    residual = src
    for step in range(ITERS):
        lo_i = shifted(state[:, :, ni - 1], "ia", 1)[:, None, :]
        hi_i = shifted(state[:, :, 0], "ia", -1)[:, None, :]
        lo_j = shifted(state[:, nj - 1 :, :], "ja", 1)
        hi_j = shifted(state[:, :1, :], "ja", -1)
        lo_k = shifted(state, "ka", 1)
        hi_k = shifted(state, "ka", -1)
        residual, plain_i = res_call(
            state, src, diag, wi[0], wj[0], wk[0], lo_i, hi_i, lo_j, hi_j, lo_k, hi_k, eigvec_inv, dinv_i_t
        )
        ends_i = jnp.stack([plain_i[:, :, width - 2], plain_i[:, :, width - 1]])
        in_i = inbound_ends(ends_i, pow_i, "ia")
        plain_j = across_call(
            plain_i, in_i[0][:, None, :], in_i[1][:, None, :], first_i_row, last_i_row, block_inv_j
        )
        ends_j = jnp.stack([plain_j[:, width - 2, :], plain_j[:, width - 1, :]])
        in_j = inbound_ends(ends_j, pow_j, "ja")
        state = update_call(
            state, plain_j, in_j[0][:, None, :], in_j[1][:, None, :], first_j_col, last_j_col, eigvec
        )
    return (state.reshape(adjoint.shape), residual.reshape(adjoint.shape))


def solution(mesh):
    return jax.shard_map(
        local,
        mesh=mesh,
        in_specs=(
            P(None, "ka", "ja", "ia"),
            P(None, "ka", "ja", "ia"),
            P(None, "ka", "ja", "ia"),
            P("ka", "ja", "ia"),
            P("ka", "ja", "ia"),
            P("ka", "ja", "ia"),
            P(),
            P(),
            P(),
            P(),
            P(),
            P(),
        ),
        out_specs=(P(None, "ka", "ja", "ia"), P(None, "ka", "ja", "ia")),
        check_vma=False,
    )
```

```python
import jax
import jax.numpy as jnp
from jax import lax
from jax.experimental import pallas as pl
from jax.experimental.pallas import tpu as pltpu
from jax.sharding import PartitionSpec as P

ITERS = 2
HI = lax.Precision.HIGHEST


def shifted(value, axis, by):
    length = lax.axis_size(axis)
    pairs = [(i, i + by) for i in range(length) if 0 <= i + by < length]
    return lax.ppermute(value, axis, pairs)


def inflow_terms(dinv, band):
    coef_one = band[:, 0][:, None]
    coef_two = band[:, 1][:, None]
    resp_last = -(coef_one * dinv[:, :, 0] + coef_two * dinv[:, :, 1])
    resp_first = -coef_two * dinv[:, :, 0]
    return resp_first, resp_last


def carry_step(resp_first, resp_last):
    width = resp_first.shape[-1]
    top = jnp.stack([resp_first[:, width - 2], resp_last[:, width - 2]])
    bottom = jnp.stack([resp_first[:, width - 1], resp_last[:, width - 1]])
    return jnp.stack([top, bottom])


def _vmem():
    return pl.BlockSpec(memory_space=pltpu.VMEM)


def _smem():
    return pl.BlockSpec(memory_space=pltpu.SMEM)


def _mm(a, b):
    return jnp.dot(a, b, precision=HI, preferred_element_type=jnp.float32)


def _column(vec, shape):
    return jnp.transpose(jnp.broadcast_to(vec, (shape[1], shape[0])))


def residual_kernel(state, src, diag, wi, wj, wk, lo_i, hi_i, lo_j, hi_j, lo_k, hi_k, mix, dinv_t,
                    res_out, plain_out, ends_out, chars):
    nv, nj, ni = state.shape
    lane = lax.broadcasted_iota(jnp.int32, (nj, ni), 1)
    row = lax.broadcasted_iota(jnp.int32, (nj, ni), 0)
    for v in range(nv):
        x = state[v]
        right_i = jnp.where(lane == ni - 1, _column(hi_i[v : v + 1, :], (nj, ni)), pltpu.roll(x, ni - 1, 1))
        left_i = jnp.where(lane == 0, _column(lo_i[v : v + 1, :], (nj, ni)), pltpu.roll(x, 1, 1))
        up_j = jnp.where(row == nj - 1, hi_j[v : v + 1, :], pltpu.roll(x, nj - 1, 0))
        down_j = jnp.where(row == 0, lo_j[v : v + 1, :], pltpu.roll(x, 1, 0))
        res_out[v] = (
            src[v]
            - diag[v] * x
            + wi[...] * (right_i + left_i)
            + wj[...] * (up_j + down_j)
            + wk[...] * (hi_k[v] + lo_k[v])
        )
    for u in range(nv):
        acc = mix[u, 0] * res_out[0]
        for v in range(1, nv):
            acc = acc + mix[u, v] * res_out[v]
        chars[u] = acc
    for u in range(nv):
        plain = _mm(chars[u], dinv_t[u])
        plain_out[u] = plain
        turned = jnp.transpose(plain)
        ends_out[0, u : u + 1, :] = turned[ni - 2 : ni - 1, :]
        ends_out[1, u : u + 1, :] = turned[ni - 1 : ni, :]


def _inbound(gathered, step, me):
    zero = jnp.zeros(gathered.shape[2:], jnp.float32)

    def body(c, carry):
        e0, e1 = carry
        n0 = step[0, 0] * e0 + step[0, 1] * e1 + gathered[c, 0]
        n1 = step[1, 0] * e0 + step[1, 1] * e1 + gathered[c, 1]
        return n0, n1

    return lax.fori_loop(0, me, body, (zero, zero))


def across_i_kernel(me, plain, gathered, step, first, last, dinv, out, ends_out):
    nv, nj, ni = plain.shape
    in_first, in_last = _inbound(gathered, step, me[0])
    for v in range(nv):
        fixed = (
            plain[v]
            + _column(in_first[v : v + 1, :], (nj, ni)) * first[v : v + 1, :]
            + _column(in_last[v : v + 1, :], (nj, ni)) * last[v : v + 1, :]
        )
        solved = _mm(dinv[v], fixed)
        out[v] = solved
        ends_out[0, v : v + 1, :] = solved[nj - 2 : nj - 1, :]
        ends_out[1, v : v + 1, :] = solved[nj - 1 : nj, :]


def update_kernel(me, state, plain, gathered, step, first, last, mix, out, lo_i, hi_i, lo_j, hi_j, chars):
    nv, nj, ni = plain.shape
    in_first, in_last = _inbound(gathered, step, me[0])
    for v in range(nv):
        chars[v] = (
            plain[v]
            + in_first[v : v + 1, :] * _column(first[v : v + 1, :], (nj, ni))
            + in_last[v : v + 1, :] * _column(last[v : v + 1, :], (nj, ni))
        )
    for u in range(nv):
        total = mix[u, 0] * chars[0]
        for v in range(1, nv):
            total = total + mix[u, v] * chars[v]
        new = state[u] + total
        out[u] = new
        turned = jnp.transpose(new)
        lo_i[u : u + 1, :] = turned[ni - 1 : ni, :]
        hi_i[u : u + 1, :] = turned[0:1, :]
        lo_j[u : u + 1, :] = new[nj - 1 : nj, :]
        hi_j[u : u + 1, :] = new[0:1, :]


def _call(kernel, n_in, smem_at, outs, scratch):
    specs = [_smem() if k in smem_at else _vmem() for k in range(n_in)]
    return pl.pallas_call(
        kernel,
        out_shape=outs,
        in_specs=specs,
        out_specs=tuple(_vmem() for _ in outs) if isinstance(outs, tuple) else _vmem(),
        scratch_shapes=scratch,
    )


def local(
    adjoint,
    source,
    diagonal,
    weight_i,
    weight_j,
    weight_k,
    eigvec,
    eigvec_inv,
    block_inv_i,
    block_inv_j,
    band_i,
    band_j,
):
    nv = adjoint.shape[0]
    nj, ni = adjoint.shape[2], adjoint.shape[3]
    width = block_inv_i.shape[-1]
    state = adjoint.reshape(nv, nj, ni)
    src = source.reshape(nv, nj, ni)
    diag = diagonal.reshape(nv, nj, ni)
    wi = weight_i.reshape(1, nj, ni)
    wj = weight_j.reshape(1, nj, ni)
    wk = weight_k.reshape(1, nj, ni)

    first_i, last_i = inflow_terms(block_inv_i, band_i)
    first_j, last_j = inflow_terms(block_inv_j, band_j)

    blk = jax.ShapeDtypeStruct((nv, nj, ni), jnp.float32)
    ends = jax.ShapeDtypeStruct((2, nv, ni), jnp.float32)
    face = jax.ShapeDtypeStruct((nv, ni), jnp.float32)
    scratch = [pltpu.VMEM((nv, nj, ni), jnp.float32)]
    res_call = _call(residual_kernel, 14, (12,), (blk, blk, ends), scratch)
    across_call = _call(across_i_kernel, 7, (0,), (blk, ends), [])
    update_call = _call(update_kernel, 8, (0, 7), (blk, face, face, face, face), scratch)
    dinv_i_t = jnp.swapaxes(block_inv_i, 1, 2)
    step_i = jnp.broadcast_to(carry_step(first_i, last_i)[:, :, :, None], (2, 2, nv, nj))
    step_j = jnp.broadcast_to(carry_step(first_j, last_j)[:, :, :, None], (2, 2, nv, ni))
    me_i = lax.axis_index("ia").astype(jnp.int32).reshape(1)
    me_j = lax.axis_index("ja").astype(jnp.int32).reshape(1)

    residual = src
    faces = (state[:, :, ni - 1], state[:, :, 0], state[:, nj - 1, :], state[:, 0, :])
    for step in range(ITERS):
        lo_i = shifted(faces[0], "ia", 1)
        hi_i = shifted(faces[1], "ia", -1)
        lo_j = shifted(faces[2], "ja", 1)
        hi_j = shifted(faces[3], "ja", -1)
        lo_k = shifted(state, "ka", 1)
        hi_k = shifted(state, "ka", -1)
        residual, plain_i, ends_i = res_call(
            state, src, diag, wi[0], wj[0], wk[0], lo_i, hi_i, lo_j, hi_j, lo_k, hi_k, eigvec_inv, dinv_i_t
        )
        gathered_i = lax.all_gather(ends_i, "ia")
        plain_j, ends_j = across_call(me_i, plain_i, gathered_i, step_i, first_i, last_i, block_inv_j)
        gathered_j = lax.all_gather(ends_j, "ja")
        state, *faces = update_call(me_j, state, plain_j, gathered_j, step_j, first_j, last_j, eigvec)
    return (state.reshape(adjoint.shape), residual.reshape(adjoint.shape))


def solution(mesh):
    return jax.shard_map(
        local,
        mesh=mesh,
        in_specs=(
            P(None, "ka", "ja", "ia"),
            P(None, "ka", "ja", "ia"),
            P(None, "ka", "ja", "ia"),
            P("ka", "ja", "ia"),
            P("ka", "ja", "ia"),
            P("ka", "ja", "ia"),
            P(),
            P(),
            P(),
            P(),
            P(),
            P(),
        ),
        out_specs=(P(None, "ka", "ja", "ia"), P(None, "ka", "ja", "ia")),
        check_vma=False,
    )
```

```python
import jax
import jax.numpy as jnp
from jax import lax
from jax.experimental import pallas as pl
from jax.experimental.pallas import tpu as pltpu
from jax.sharding import PartitionSpec as P

ITERS = 2
HI = lax.Precision.HIGHEST


def shifted(value, axis, by):
    length = lax.axis_size(axis)
    pairs = [(i, i + by) for i in range(length) if 0 <= i + by < length]
    return lax.ppermute(value, axis, pairs)


def inflow_terms(dinv, band):
    coef_one = band[:, 0][:, None]
    coef_two = band[:, 1][:, None]
    resp_last = -(coef_one * dinv[:, :, 0] + coef_two * dinv[:, :, 1])
    resp_first = -coef_two * dinv[:, :, 0]
    return resp_first, resp_last


def carry_step(resp_first, resp_last):
    width = resp_first.shape[-1]
    top = jnp.stack([resp_first[:, width - 2], resp_last[:, width - 2]])
    bottom = jnp.stack([resp_first[:, width - 1], resp_last[:, width - 1]])
    return jnp.stack([top, bottom])


def gather_ends(ends, axis):
    count = lax.axis_size(axis)
    copies = jnp.broadcast_to(ends[None], (count,) + ends.shape)
    return lax.all_to_all(copies, axis, 0, 0, tiled=True)


def _vmem():
    return pl.BlockSpec(memory_space=pltpu.VMEM)


def _smem():
    return pl.BlockSpec(memory_space=pltpu.SMEM)


def _mm(a, b):
    return jnp.dot(a, b, precision=HI, preferred_element_type=jnp.float32)


def _column(vec, shape):
    return jnp.transpose(jnp.broadcast_to(vec, (shape[1], shape[0])))


def residual_kernel(state, src, diag, wi, wj, wk, lo_i, hi_i, lo_j, hi_j, lo_k, hi_k, mix, dinv_t,
                    res_out, plain_out, ends_out, chars):
    nv, nj, ni = state.shape
    lane = lax.broadcasted_iota(jnp.int32, (nj, ni), 1)
    row = lax.broadcasted_iota(jnp.int32, (nj, ni), 0)
    for v in range(nv):
        x = state[v]
        right_i = jnp.where(lane == ni - 1, _column(hi_i[v : v + 1, :], (nj, ni)), pltpu.roll(x, ni - 1, 1))
        left_i = jnp.where(lane == 0, _column(lo_i[v : v + 1, :], (nj, ni)), pltpu.roll(x, 1, 1))
        up_j = jnp.where(row == nj - 1, hi_j[v : v + 1, :], pltpu.roll(x, nj - 1, 0))
        down_j = jnp.where(row == 0, lo_j[v : v + 1, :], pltpu.roll(x, 1, 0))
        res_out[v] = (
            src[v]
            - diag[v] * x
            + wi[...] * (right_i + left_i)
            + wj[...] * (up_j + down_j)
            + wk[...] * (hi_k[v] + lo_k[v])
        )
    for u in range(nv):
        acc = mix[u, 0] * res_out[0]
        for v in range(1, nv):
            acc = acc + mix[u, v] * res_out[v]
        chars[u] = acc
    for u in range(nv):
        plain = _mm(chars[u], dinv_t[u])
        plain_out[u] = plain
        turned = jnp.transpose(plain)
        ends_out[0, u : u + 1, :] = turned[ni - 2 : ni - 1, :]
        ends_out[1, u : u + 1, :] = turned[ni - 1 : ni, :]


def _inbound(gathered, step, me):
    zero = jnp.zeros(gathered.shape[2:], jnp.float32)

    def body(c, carry):
        e0, e1 = carry
        n0 = step[0, 0] * e0 + step[0, 1] * e1 + gathered[c, 0]
        n1 = step[1, 0] * e0 + step[1, 1] * e1 + gathered[c, 1]
        return n0, n1

    return lax.fori_loop(0, me, body, (zero, zero))


def across_i_kernel(me, plain, gathered, step, first, last, dinv, out, ends_out):
    nv, nj, ni = plain.shape
    in_first, in_last = _inbound(gathered, step, me[0])
    for v in range(nv):
        fixed = (
            plain[v]
            + _column(in_first[v : v + 1, :], (nj, ni)) * first[v : v + 1, :]
            + _column(in_last[v : v + 1, :], (nj, ni)) * last[v : v + 1, :]
        )
        solved = _mm(dinv[v], fixed)
        out[v] = solved
        ends_out[0, v : v + 1, :] = solved[nj - 2 : nj - 1, :]
        ends_out[1, v : v + 1, :] = solved[nj - 1 : nj, :]


def update_kernel(me, state, plain, gathered, step, first, last, mix, out, lo_i, hi_i, lo_j, hi_j, chars):
    nv, nj, ni = plain.shape
    in_first, in_last = _inbound(gathered, step, me[0])
    for v in range(nv):
        chars[v] = (
            plain[v]
            + in_first[v : v + 1, :] * _column(first[v : v + 1, :], (nj, ni))
            + in_last[v : v + 1, :] * _column(last[v : v + 1, :], (nj, ni))
        )
    for u in range(nv):
        total = mix[u, 0] * chars[0]
        for v in range(1, nv):
            total = total + mix[u, v] * chars[v]
        new = state[u] + total
        out[u] = new
        turned = jnp.transpose(new)
        lo_i[u : u + 1, :] = turned[ni - 1 : ni, :]
        hi_i[u : u + 1, :] = turned[0:1, :]
        lo_j[u : u + 1, :] = new[nj - 1 : nj, :]
        hi_j[u : u + 1, :] = new[0:1, :]


def _call(kernel, n_in, smem_at, outs, scratch):
    specs = [_smem() if k in smem_at else _vmem() for k in range(n_in)]
    return pl.pallas_call(
        kernel,
        out_shape=outs,
        in_specs=specs,
        out_specs=tuple(_vmem() for _ in outs) if isinstance(outs, tuple) else _vmem(),
        scratch_shapes=scratch,
    )


def local(
    adjoint,
    source,
    diagonal,
    weight_i,
    weight_j,
    weight_k,
    eigvec,
    eigvec_inv,
    block_inv_i,
    block_inv_j,
    band_i,
    band_j,
):
    nv = adjoint.shape[0]
    nj, ni = adjoint.shape[2], adjoint.shape[3]
    width = block_inv_i.shape[-1]
    state = adjoint.reshape(nv, nj, ni)
    src = source.reshape(nv, nj, ni)
    diag = diagonal.reshape(nv, nj, ni)
    wi = weight_i.reshape(1, nj, ni)
    wj = weight_j.reshape(1, nj, ni)
    wk = weight_k.reshape(1, nj, ni)

    first_i, last_i = inflow_terms(block_inv_i, band_i)
    first_j, last_j = inflow_terms(block_inv_j, band_j)

    blk = jax.ShapeDtypeStruct((nv, nj, ni), jnp.float32)
    ends = jax.ShapeDtypeStruct((2, nv, ni), jnp.float32)
    face = jax.ShapeDtypeStruct((nv, ni), jnp.float32)
    scratch = [pltpu.VMEM((nv, nj, ni), jnp.float32)]
    res_call = _call(residual_kernel, 14, (12,), (blk, blk, ends), scratch)
    across_call = _call(across_i_kernel, 7, (0,), (blk, ends), [])
    update_call = _call(update_kernel, 8, (0, 7), (blk, face, face, face, face), scratch)
    dinv_i_t = jnp.swapaxes(block_inv_i, 1, 2)
    step_i = jnp.broadcast_to(carry_step(first_i, last_i)[:, :, :, None], (2, 2, nv, nj))
    step_j = jnp.broadcast_to(carry_step(first_j, last_j)[:, :, :, None], (2, 2, nv, ni))
    me_i = lax.axis_index("ia").astype(jnp.int32).reshape(1)
    me_j = lax.axis_index("ja").astype(jnp.int32).reshape(1)

    residual = src
    faces = (state[:, :, ni - 1], state[:, :, 0], state[:, nj - 1, :], state[:, 0, :])
    for step in range(ITERS):
        lo_i = shifted(faces[0], "ia", 1)
        hi_i = shifted(faces[1], "ia", -1)
        lo_j = shifted(faces[2], "ja", 1)
        hi_j = shifted(faces[3], "ja", -1)
        lo_k = shifted(state, "ka", 1)
        hi_k = shifted(state, "ka", -1)
        residual, plain_i, ends_i = res_call(
            state, src, diag, wi[0], wj[0], wk[0], lo_i, hi_i, lo_j, hi_j, lo_k, hi_k, eigvec_inv, dinv_i_t
        )
        gathered_i = gather_ends(ends_i, "ia")
        plain_j, ends_j = across_call(me_i, plain_i, gathered_i, step_i, first_i, last_i, block_inv_j)
        gathered_j = gather_ends(ends_j, "ja")
        state, *faces = update_call(me_j, state, plain_j, gathered_j, step_j, first_j, last_j, eigvec)
    return (state.reshape(adjoint.shape), residual.reshape(adjoint.shape))


def solution(mesh):
    return jax.shard_map(
        local,
        mesh=mesh,
        in_specs=(
            P(None, "ka", "ja", "ia"),
            P(None, "ka", "ja", "ia"),
            P(None, "ka", "ja", "ia"),
            P("ka", "ja", "ia"),
            P("ka", "ja", "ia"),
            P("ka", "ja", "ia"),
            P(),
            P(),
            P(),
            P(),
            P(),
            P(),
        ),
        out_specs=(P(None, "ka", "ja", "ia"), P(None, "ka", "ja", "ia")),
        check_vma=False,
    )
```

```python
import jax
import jax.numpy as jnp
from jax import lax
from jax.experimental import pallas as pl
from jax.experimental.pallas import tpu as pltpu
from jax.sharding import PartitionSpec as P

ITERS = 2
HI = lax.Precision.HIGHEST


def shifted(value, axis, by):
    length = lax.axis_size(axis)
    pairs = [(i, i + by) for i in range(length) if 0 <= i + by < length]
    return lax.ppermute(value, axis, pairs)


def inflow_terms(dinv, band):
    coef_one = band[:, 0][:, None]
    coef_two = band[:, 1][:, None]
    resp_last = -(coef_one * dinv[:, :, 0] + coef_two * dinv[:, :, 1])
    resp_first = -coef_two * dinv[:, :, 0]
    return resp_first, resp_last


def carry_step(resp_first, resp_last):
    width = resp_first.shape[-1]
    top = jnp.stack([resp_first[:, width - 2], resp_last[:, width - 2]])
    bottom = jnp.stack([resp_first[:, width - 1], resp_last[:, width - 1]])
    return jnp.stack([top, bottom])


def gather_ends(copies, axis):
    return lax.all_to_all(copies, axis, 0, 0, tiled=True)


def _vmem():
    return pl.BlockSpec(memory_space=pltpu.VMEM)


def _smem():
    return pl.BlockSpec(memory_space=pltpu.SMEM)


def _mm(a, b):
    return jnp.dot(a, b, precision=HI, preferred_element_type=jnp.float32)


def _stack_rows(rows, height):
    row = lax.broadcasted_iota(jnp.int32, (height, rows[0].shape[-1]), 0)
    tile = jnp.zeros((height, rows[0].shape[-1]), jnp.float32)
    for k, r in enumerate(rows):
        tile = jnp.where(row == k, r, tile)
    return tile


def _emit_copies(ends_out, first_rows, last_rows):
    top = _stack_rows(first_rows, 8)
    bottom = _stack_rows(last_rows, 8)
    for c in range(ends_out.shape[0]):
        ends_out[c, 0:8, :] = top
        ends_out[c, 8:16, :] = bottom


def _coef(step, a, d, nv, n):
    row = lax.broadcasted_iota(jnp.int32, (8, n), 0)
    tile = jnp.zeros((8, n), jnp.float32)
    for v in range(nv):
        tile = jnp.where(row == v, step[(a * 2 + d) * nv + v], tile)
    return tile


def _column(vec, shape):
    return jnp.transpose(jnp.broadcast_to(vec, (shape[1], shape[0])))


def residual_kernel(state, src, diag, wi, wj, wk, lo_i, hi_i, lo_j, hi_j, lo_k, hi_k, mix, dinv_t,
                    res_out, plain_out, ends_out, chars):
    nv, nj, ni = state.shape
    lane = lax.broadcasted_iota(jnp.int32, (nj, ni), 1)
    row = lax.broadcasted_iota(jnp.int32, (nj, ni), 0)
    for v in range(nv):
        x = state[v]
        right_i = jnp.where(lane == ni - 1, _column(hi_i[v : v + 1, :], (nj, ni)), pltpu.roll(x, ni - 1, 1))
        left_i = jnp.where(lane == 0, _column(lo_i[v : v + 1, :], (nj, ni)), pltpu.roll(x, 1, 1))
        up_j = jnp.where(row == nj - 1, hi_j[v : v + 1, :], pltpu.roll(x, nj - 1, 0))
        down_j = jnp.where(row == 0, lo_j[v : v + 1, :], pltpu.roll(x, 1, 0))
        res_out[v] = (
            src[v]
            - diag[v] * x
            + wi[...] * (right_i + left_i)
            + wj[...] * (up_j + down_j)
            + wk[...] * (hi_k[v] + lo_k[v])
        )
    for u in range(nv):
        acc = mix[u, 0] * res_out[0]
        for v in range(1, nv):
            acc = acc + mix[u, v] * res_out[v]
        chars[u] = acc
    first_rows, last_rows = [], []
    for u in range(nv):
        plain = _mm(chars[u], dinv_t[u])
        plain_out[u] = plain
        turned = jnp.transpose(plain)
        first_rows.append(turned[ni - 2 : ni - 1, :])
        last_rows.append(turned[ni - 1 : ni, :])
    _emit_copies(ends_out, first_rows, last_rows)


def _inbound(gathered, step, me, nv):
    n = gathered.shape[-1]
    zero = jnp.zeros((8, n), jnp.float32)
    m00, m01 = _coef(step, 0, 0, nv, n), _coef(step, 0, 1, nv, n)
    m10, m11 = _coef(step, 1, 0, nv, n), _coef(step, 1, 1, nv, n)

    def body(c, carry):
        e0, e1 = carry
        n0 = m00 * e0 + m01 * e1 + gathered[c, 0:8, :]
        n1 = m10 * e0 + m11 * e1 + gathered[c, 8:16, :]
        return n0, n1

    return lax.fori_loop(0, me, body, (zero, zero))


def across_i_kernel(me, plain, gathered, step, first, last, dinv, out, ends_out):
    nv, nj, ni = plain.shape
    in_first, in_last = _inbound(gathered, step, me[0], nv)
    first_rows, last_rows = [], []
    for v in range(nv):
        fixed = (
            plain[v]
            + _column(in_first[v : v + 1, :], (nj, ni)) * first[v : v + 1, :]
            + _column(in_last[v : v + 1, :], (nj, ni)) * last[v : v + 1, :]
        )
        solved = _mm(dinv[v], fixed)
        out[v] = solved
        first_rows.append(solved[nj - 2 : nj - 1, :])
        last_rows.append(solved[nj - 1 : nj, :])
    _emit_copies(ends_out, first_rows, last_rows)


def update_kernel(me, state, plain, gathered, step, first, last, mix, out, lo_i, hi_i, lo_j, hi_j, chars):
    nv, nj, ni = plain.shape
    in_first, in_last = _inbound(gathered, step, me[0], nv)
    for v in range(nv):
        chars[v] = (
            plain[v]
            + in_first[v : v + 1, :] * _column(first[v : v + 1, :], (nj, ni))
            + in_last[v : v + 1, :] * _column(last[v : v + 1, :], (nj, ni))
        )
    for u in range(nv):
        total = mix[u, 0] * chars[0]
        for v in range(1, nv):
            total = total + mix[u, v] * chars[v]
        new = state[u] + total
        out[u] = new
        turned = jnp.transpose(new)
        lo_i[u : u + 1, :] = turned[ni - 1 : ni, :]
        hi_i[u : u + 1, :] = turned[0:1, :]
        lo_j[u : u + 1, :] = new[nj - 1 : nj, :]
        hi_j[u : u + 1, :] = new[0:1, :]


def _call(kernel, n_in, smem_at, outs, scratch):
    specs = [_smem() if k in smem_at else _vmem() for k in range(n_in)]
    return pl.pallas_call(
        kernel,
        out_shape=outs,
        in_specs=specs,
        out_specs=tuple(_vmem() for _ in outs) if isinstance(outs, tuple) else _vmem(),
        scratch_shapes=scratch,
    )


def local(
    adjoint,
    source,
    diagonal,
    weight_i,
    weight_j,
    weight_k,
    eigvec,
    eigvec_inv,
    block_inv_i,
    block_inv_j,
    band_i,
    band_j,
):
    nv = adjoint.shape[0]
    nj, ni = adjoint.shape[2], adjoint.shape[3]
    width = block_inv_i.shape[-1]
    state = adjoint.reshape(nv, nj, ni)
    src = source.reshape(nv, nj, ni)
    diag = diagonal.reshape(nv, nj, ni)
    wi = weight_i.reshape(1, nj, ni)
    wj = weight_j.reshape(1, nj, ni)
    wk = weight_k.reshape(1, nj, ni)

    first_i, last_i = inflow_terms(block_inv_i, band_i)
    first_j, last_j = inflow_terms(block_inv_j, band_j)

    blk = jax.ShapeDtypeStruct((nv, nj, ni), jnp.float32)
    ends_i = jax.ShapeDtypeStruct((lax.axis_size("ia"), 16, nj), jnp.float32)
    ends_j = jax.ShapeDtypeStruct((lax.axis_size("ja"), 16, ni), jnp.float32)
    face = jax.ShapeDtypeStruct((nv, ni), jnp.float32)
    scratch = [pltpu.VMEM((nv, nj, ni), jnp.float32)]
    res_call = _call(residual_kernel, 14, (12,), (blk, blk, ends_i), scratch)
    across_call = _call(across_i_kernel, 7, (0, 3), (blk, ends_j), [])
    update_call = _call(update_kernel, 8, (0, 4, 7), (blk, face, face, face, face), scratch)
    dinv_i_t = jnp.swapaxes(block_inv_i, 1, 2)
    step_i = carry_step(first_i, last_i).reshape(-1)
    step_j = carry_step(first_j, last_j).reshape(-1)
    me_i = lax.axis_index("ia").astype(jnp.int32).reshape(1)
    me_j = lax.axis_index("ja").astype(jnp.int32).reshape(1)

    residual = src
    faces = (state[:, :, ni - 1], state[:, :, 0], state[:, nj - 1, :], state[:, 0, :])
    for step in range(ITERS):
        lo_i = shifted(faces[0], "ia", 1)
        hi_i = shifted(faces[1], "ia", -1)
        lo_j = shifted(faces[2], "ja", 1)
        hi_j = shifted(faces[3], "ja", -1)
        lo_k = shifted(state, "ka", 1)
        hi_k = shifted(state, "ka", -1)
        residual, plain_i, ends_i = res_call(
            state, src, diag, wi[0], wj[0], wk[0], lo_i, hi_i, lo_j, hi_j, lo_k, hi_k, eigvec_inv, dinv_i_t
        )
        gathered_i = gather_ends(ends_i, "ia")
        plain_j, ends_j = across_call(me_i, plain_i, gathered_i, step_i, first_i, last_i, block_inv_j)
        gathered_j = gather_ends(ends_j, "ja")
        state, *faces = update_call(me_j, state, plain_j, gathered_j, step_j, first_j, last_j, eigvec)
    return (state.reshape(adjoint.shape), residual.reshape(adjoint.shape))


def solution(mesh):
    return jax.shard_map(
        local,
        mesh=mesh,
        in_specs=(
            P(None, "ka", "ja", "ia"),
            P(None, "ka", "ja", "ia"),
            P(None, "ka", "ja", "ia"),
            P("ka", "ja", "ia"),
            P("ka", "ja", "ia"),
            P("ka", "ja", "ia"),
            P(),
            P(),
            P(),
            P(),
            P(),
            P(),
        ),
        out_specs=(P(None, "ka", "ja", "ia"), P(None, "ka", "ja", "ia")),
        check_vma=False,
    )
```

```python
import jax
import jax.numpy as jnp
from jax import lax
from jax.experimental import pallas as pl
from jax.experimental.pallas import tpu as pltpu
from jax.sharding import PartitionSpec as P

ITERS = 2
HI = lax.Precision.HIGHEST


def shifted(value, axis, by):
    length = lax.axis_size(axis)
    pairs = [(i, i + by) for i in range(length) if 0 <= i + by < length]
    return lax.ppermute(value, axis, pairs)


def inflow_terms(dinv, band):
    coef_one = band[:, 0][:, None]
    coef_two = band[:, 1][:, None]
    resp_last = -(coef_one * dinv[:, :, 0] + coef_two * dinv[:, :, 1])
    resp_first = -coef_two * dinv[:, :, 0]
    return resp_first, resp_last


def carry_step(resp_first, resp_last):
    width = resp_first.shape[-1]
    top = jnp.stack([resp_first[:, width - 2], resp_last[:, width - 2]])
    bottom = jnp.stack([resp_first[:, width - 1], resp_last[:, width - 1]])
    return jnp.stack([top, bottom])


def gather_ends(copies, axis):
    return lax.all_to_all(copies, axis, 0, 0, tiled=True)


def _vmem():
    return pl.BlockSpec(memory_space=pltpu.VMEM)


def _smem():
    return pl.BlockSpec(memory_space=pltpu.SMEM)


def _mm(a, b):
    return jnp.dot(a, b, precision=HI, preferred_element_type=jnp.float32)


def _stack_rows(rows, height):
    row = lax.broadcasted_iota(jnp.int32, (height, rows[0].shape[-1]), 0)
    tile = jnp.zeros((height, rows[0].shape[-1]), jnp.float32)
    for k, r in enumerate(rows):
        tile = jnp.where(row == k, r, tile)
    return tile


def _emit_copies(ends_out, first_rows, last_rows):
    top = _stack_rows(first_rows, 8)
    bottom = _stack_rows(last_rows, 8)
    for c in range(ends_out.shape[0]):
        ends_out[c, 0:8, :] = top
        ends_out[c, 8:16, :] = bottom


def _coef(step, a, d, nv, n):
    row = lax.broadcasted_iota(jnp.int32, (8, n), 0)
    tile = jnp.zeros((8, n), jnp.float32)
    for v in range(nv):
        tile = jnp.where(row == v, step[(a * 2 + d) * nv + v], tile)
    return tile


def _column(vec, shape):
    return jnp.transpose(jnp.broadcast_to(vec, (shape[1], shape[0])))


def residual_kernel(state, src, diag, wi, wj, wk, lo_i, hi_i, lo_j, hi_j, lo_k, hi_k, mix, dinv,
                    res_out, plain_out, ends_out, chars):
    nv, nj, ni = state.shape
    lane = lax.broadcasted_iota(jnp.int32, (nj, ni), 1)
    row = lax.broadcasted_iota(jnp.int32, (nj, ni), 0)
    for v in range(nv):
        x = state[v]
        right_i = jnp.where(lane == ni - 1, _column(hi_i[v : v + 1, :], (nj, ni)), pltpu.roll(x, ni - 1, 1))
        left_i = jnp.where(lane == 0, _column(lo_i[v : v + 1, :], (nj, ni)), pltpu.roll(x, 1, 1))
        up_j = jnp.where(row == nj - 1, hi_j[v : v + 1, :], pltpu.roll(x, nj - 1, 0))
        down_j = jnp.where(row == 0, lo_j[v : v + 1, :], pltpu.roll(x, 1, 0))
        res_out[v] = (
            src[v]
            - diag[v] * x
            + wi[...] * (right_i + left_i)
            + wj[...] * (up_j + down_j)
            + wk[...] * (hi_k[v] + lo_k[v])
        )
    for u in range(nv):
        acc = mix[u, 0] * res_out[0]
        for v in range(1, nv):
            acc = acc + mix[u, v] * res_out[v]
        chars[u] = acc
    first_rows, last_rows = [], []
    for u in range(nv):
        plain = lax.dot_general(
            chars[u], dinv[u], (((1,), (1,)), ((), ())), precision=HI, preferred_element_type=jnp.float32
        )
        plain_out[u] = plain
        turned = jnp.transpose(plain)
        first_rows.append(turned[ni - 2 : ni - 1, :])
        last_rows.append(turned[ni - 1 : ni, :])
    _emit_copies(ends_out, first_rows, last_rows)


def _inbound(gathered, step, me, nv):
    n = gathered.shape[-1]
    zero = jnp.zeros((8, n), jnp.float32)
    m00, m01 = _coef(step, 0, 0, nv, n), _coef(step, 0, 1, nv, n)
    m10, m11 = _coef(step, 1, 0, nv, n), _coef(step, 1, 1, nv, n)

    def body(c, carry):
        e0, e1 = carry
        n0 = m00 * e0 + m01 * e1 + gathered[c, 0:8, :]
        n1 = m10 * e0 + m11 * e1 + gathered[c, 8:16, :]
        return n0, n1

    return lax.fori_loop(0, me, body, (zero, zero))


def across_i_kernel(me, plain, gathered, step, first, last, dinv, out, ends_out):
    nv, nj, ni = plain.shape
    in_first, in_last = _inbound(gathered, step, me[0], nv)
    first_rows, last_rows = [], []
    for v in range(nv):
        fixed = (
            plain[v]
            + _column(in_first[v : v + 1, :], (nj, ni)) * first[v : v + 1, :]
            + _column(in_last[v : v + 1, :], (nj, ni)) * last[v : v + 1, :]
        )
        solved = _mm(dinv[v], fixed)
        out[v] = solved
        first_rows.append(solved[nj - 2 : nj - 1, :])
        last_rows.append(solved[nj - 1 : nj, :])
    _emit_copies(ends_out, first_rows, last_rows)


def update_kernel(me, state, plain, gathered, step, first, last, mix, out, lo_i, hi_i, lo_j, hi_j, chars):
    nv, nj, ni = plain.shape
    in_first, in_last = _inbound(gathered, step, me[0], nv)
    for v in range(nv):
        chars[v] = (
            plain[v]
            + in_first[v : v + 1, :] * _column(first[v : v + 1, :], (nj, ni))
            + in_last[v : v + 1, :] * _column(last[v : v + 1, :], (nj, ni))
        )
    for u in range(nv):
        total = mix[u, 0] * chars[0]
        for v in range(1, nv):
            total = total + mix[u, v] * chars[v]
        new = state[u] + total
        out[u] = new
        turned = jnp.transpose(new)
        lo_i[u : u + 1, :] = turned[ni - 1 : ni, :]
        hi_i[u : u + 1, :] = turned[0:1, :]
        lo_j[u : u + 1, :] = new[nj - 1 : nj, :]
        hi_j[u : u + 1, :] = new[0:1, :]


def _call(kernel, n_in, smem_at, outs, scratch):
    specs = [_smem() if k in smem_at else _vmem() for k in range(n_in)]
    return pl.pallas_call(
        kernel,
        out_shape=outs,
        in_specs=specs,
        out_specs=tuple(_vmem() for _ in outs) if isinstance(outs, tuple) else _vmem(),
        scratch_shapes=scratch,
    )


def local(
    adjoint,
    source,
    diagonal,
    weight_i,
    weight_j,
    weight_k,
    eigvec,
    eigvec_inv,
    block_inv_i,
    block_inv_j,
    band_i,
    band_j,
):
    nv = adjoint.shape[0]
    nj, ni = adjoint.shape[2], adjoint.shape[3]
    width = block_inv_i.shape[-1]
    state = adjoint.reshape(nv, nj, ni)
    src = source.reshape(nv, nj, ni)
    diag = diagonal.reshape(nv, nj, ni)
    wi = weight_i.reshape(1, nj, ni)
    wj = weight_j.reshape(1, nj, ni)
    wk = weight_k.reshape(1, nj, ni)

    first_i, last_i = inflow_terms(block_inv_i, band_i)
    first_j, last_j = inflow_terms(block_inv_j, band_j)

    blk = jax.ShapeDtypeStruct((nv, nj, ni), jnp.float32)
    ends_i = jax.ShapeDtypeStruct((lax.axis_size("ia"), 16, nj), jnp.float32)
    ends_j = jax.ShapeDtypeStruct((lax.axis_size("ja"), 16, ni), jnp.float32)
    face = jax.ShapeDtypeStruct((nv, ni), jnp.float32)
    scratch = [pltpu.VMEM((nv, nj, ni), jnp.float32)]
    res_call = _call(residual_kernel, 14, (12,), (blk, blk, ends_i), scratch)
    across_call = _call(across_i_kernel, 7, (0, 3), (blk, ends_j), [])
    update_call = _call(update_kernel, 8, (0, 4, 7), (blk, face, face, face, face), scratch)
    step_i = carry_step(first_i, last_i).reshape(-1)
    step_j = carry_step(first_j, last_j).reshape(-1)
    me_i = lax.axis_index("ia").astype(jnp.int32).reshape(1)
    me_j = lax.axis_index("ja").astype(jnp.int32).reshape(1)
    src, first_i, last_i, first_j, last_j, step_i, step_j, me_i, me_j = lax.optimization_barrier(
        (src, first_i, last_i, first_j, last_j, step_i, step_j, me_i, me_j)
    )

    residual = src
    faces = (state[:, :, ni - 1], state[:, :, 0], state[:, nj - 1, :], state[:, 0, :])
    for step in range(ITERS):
        lo_i = shifted(faces[0], "ia", 1)
        hi_i = shifted(faces[1], "ia", -1)
        lo_j = shifted(faces[2], "ja", 1)
        hi_j = shifted(faces[3], "ja", -1)
        lo_k = shifted(state, "ka", 1)
        hi_k = shifted(state, "ka", -1)
        residual, plain_i, ends_i = res_call(
            state, src, diag, wi[0], wj[0], wk[0], lo_i, hi_i, lo_j, hi_j, lo_k, hi_k, eigvec_inv, block_inv_i
        )
        gathered_i = gather_ends(ends_i, "ia")
        plain_j, ends_j = across_call(me_i, plain_i, gathered_i, step_i, first_i, last_i, block_inv_j)
        gathered_j = gather_ends(ends_j, "ja")
        state, *faces = update_call(me_j, state, plain_j, gathered_j, step_j, first_j, last_j, eigvec)
    return (state.reshape(adjoint.shape), residual.reshape(adjoint.shape))


def solution(mesh):
    return jax.shard_map(
        local,
        mesh=mesh,
        in_specs=(
            P(None, "ka", "ja", "ia"),
            P(None, "ka", "ja", "ia"),
            P(None, "ka", "ja", "ia"),
            P("ka", "ja", "ia"),
            P("ka", "ja", "ia"),
            P("ka", "ja", "ia"),
            P(),
            P(),
            P(),
            P(),
            P(),
            P(),
        ),
        out_specs=(P(None, "ka", "ja", "ia"), P(None, "ka", "ja", "ia")),
        check_vma=False,
    )
```

```python
import jax
import jax.numpy as jnp
from jax import lax
from jax.experimental import pallas as pl
from jax.experimental.pallas import tpu as pltpu
from jax.sharding import PartitionSpec as P

ITERS = 2
HI = lax.Precision.HIGHEST


def shifted(value, axis, by):
    length = lax.axis_size(axis)
    pairs = [(i, i + by) for i in range(length) if 0 <= i + by < length]
    return lax.ppermute(value, axis, pairs)


def inflow_terms(dinv, band):
    coef_one = band[:, 0][:, None]
    coef_two = band[:, 1][:, None]
    resp_last = -(coef_one * dinv[:, :, 0] + coef_two * dinv[:, :, 1])
    resp_first = -coef_two * dinv[:, :, 0]
    return resp_first, resp_last


def carry_step(resp_first, resp_last):
    width = resp_first.shape[-1]
    top = jnp.stack([resp_first[:, width - 2], resp_last[:, width - 2]])
    bottom = jnp.stack([resp_first[:, width - 1], resp_last[:, width - 1]])
    return jnp.stack([top, bottom])


def gather_ends(copies, axis):
    count = lax.axis_size(axis)
    if count < 16:
        return lax.all_to_all(copies, axis, 0, 0, tiled=True)
    inner = 4
    outer = count // inner
    near = [[g * inner + r for r in range(inner)] for g in range(outer)]
    far = [[g * inner + r for g in range(outer)] for r in range(inner)]
    first = lax.all_to_all(copies[:inner], axis, 0, 0, axis_index_groups=near, tiled=True)
    spread = jnp.broadcast_to(first[None], (outer,) + first.shape)
    second = lax.all_to_all(spread, axis, 0, 0, axis_index_groups=far, tiled=True)
    return second.reshape(copies.shape)


def _vmem():
    return pl.BlockSpec(memory_space=pltpu.VMEM)


def _smem():
    return pl.BlockSpec(memory_space=pltpu.SMEM)


def _mm(a, b):
    return jnp.dot(a, b, precision=HI, preferred_element_type=jnp.float32)


def _stack_rows(rows, height):
    row = lax.broadcasted_iota(jnp.int32, (height, rows[0].shape[-1]), 0)
    tile = jnp.zeros((height, rows[0].shape[-1]), jnp.float32)
    for k, r in enumerate(rows):
        tile = jnp.where(row == k, r, tile)
    return tile


def _emit_copies(ends_out, first_rows, last_rows):
    top = _stack_rows(first_rows, 8)
    bottom = _stack_rows(last_rows, 8)
    for c in range(ends_out.shape[0]):
        ends_out[c, 0:8, :] = top
        ends_out[c, 8:16, :] = bottom


def _coef(step, a, d, nv, n):
    row = lax.broadcasted_iota(jnp.int32, (8, n), 0)
    tile = jnp.zeros((8, n), jnp.float32)
    for v in range(nv):
        tile = jnp.where(row == v, step[(a * 2 + d) * nv + v], tile)
    return tile


def _column(vec, shape):
    return jnp.transpose(jnp.broadcast_to(vec, (shape[1], shape[0])))


def residual_kernel(state, src, diag, wi, wj, wk, lo_i, hi_i, lo_j, hi_j, lo_k, hi_k, mix, dinv_t,
                    res_out, plain_out, ends_out, chars):
    nv, nj, ni = state.shape
    lane = lax.broadcasted_iota(jnp.int32, (nj, ni), 1)
    row = lax.broadcasted_iota(jnp.int32, (nj, ni), 0)
    for v in range(nv):
        x = state[v]
        right_i = jnp.where(lane == ni - 1, _column(hi_i[v : v + 1, :], (nj, ni)), pltpu.roll(x, ni - 1, 1))
        left_i = jnp.where(lane == 0, _column(lo_i[v : v + 1, :], (nj, ni)), pltpu.roll(x, 1, 1))
        up_j = jnp.where(row == nj - 1, hi_j[v : v + 1, :], pltpu.roll(x, nj - 1, 0))
        down_j = jnp.where(row == 0, lo_j[v : v + 1, :], pltpu.roll(x, 1, 0))
        res_out[v] = (
            src[v]
            - diag[v] * x
            + wi[...] * (right_i + left_i)
            + wj[...] * (up_j + down_j)
            + wk[...] * (hi_k[v] + lo_k[v])
        )
    for u in range(nv):
        acc = mix[u, 0] * res_out[0]
        for v in range(1, nv):
            acc = acc + mix[u, v] * res_out[v]
        chars[u] = acc
    first_rows, last_rows = [], []
    for u in range(nv):
        plain = _mm(chars[u], dinv_t[u])
        plain_out[u] = plain
        turned = jnp.transpose(plain)
        first_rows.append(turned[ni - 2 : ni - 1, :])
        last_rows.append(turned[ni - 1 : ni, :])
    _emit_copies(ends_out, first_rows, last_rows)


def _inbound(gathered, step, me, nv):
    n = gathered.shape[-1]
    zero = jnp.zeros((8, n), jnp.float32)
    m00, m01 = _coef(step, 0, 0, nv, n), _coef(step, 0, 1, nv, n)
    m10, m11 = _coef(step, 1, 0, nv, n), _coef(step, 1, 1, nv, n)

    def body(c, carry):
        e0, e1 = carry
        n0 = m00 * e0 + m01 * e1 + gathered[c, 0:8, :]
        n1 = m10 * e0 + m11 * e1 + gathered[c, 8:16, :]
        return n0, n1

    return lax.fori_loop(0, me, body, (zero, zero))


def across_i_kernel(me, plain, gathered, step, first, last, dinv, out, ends_out):
    nv, nj, ni = plain.shape
    in_first, in_last = _inbound(gathered, step, me[0], nv)
    first_rows, last_rows = [], []
    for v in range(nv):
        fixed = (
            plain[v]
            + _column(in_first[v : v + 1, :], (nj, ni)) * first[v : v + 1, :]
            + _column(in_last[v : v + 1, :], (nj, ni)) * last[v : v + 1, :]
        )
        solved = _mm(dinv[v], fixed)
        out[v] = solved
        first_rows.append(solved[nj - 2 : nj - 1, :])
        last_rows.append(solved[nj - 1 : nj, :])
    _emit_copies(ends_out, first_rows, last_rows)


def update_kernel(me, state, plain, gathered, step, first, last, mix, out, lo_i, hi_i, lo_j, hi_j, chars):
    nv, nj, ni = plain.shape
    in_first, in_last = _inbound(gathered, step, me[0], nv)
    for v in range(nv):
        chars[v] = (
            plain[v]
            + in_first[v : v + 1, :] * _column(first[v : v + 1, :], (nj, ni))
            + in_last[v : v + 1, :] * _column(last[v : v + 1, :], (nj, ni))
        )
    for u in range(nv):
        total = mix[u, 0] * chars[0]
        for v in range(1, nv):
            total = total + mix[u, v] * chars[v]
        new = state[u] + total
        out[u] = new
        turned = jnp.transpose(new)
        lo_i[u : u + 1, :] = turned[ni - 1 : ni, :]
        hi_i[u : u + 1, :] = turned[0:1, :]
        lo_j[u : u + 1, :] = new[nj - 1 : nj, :]
        hi_j[u : u + 1, :] = new[0:1, :]


def _call(kernel, n_in, smem_at, outs, scratch):
    specs = [_smem() if k in smem_at else _vmem() for k in range(n_in)]
    return pl.pallas_call(
        kernel,
        out_shape=outs,
        in_specs=specs,
        out_specs=tuple(_vmem() for _ in outs) if isinstance(outs, tuple) else _vmem(),
        scratch_shapes=scratch,
    )


def local(
    adjoint,
    source,
    diagonal,
    weight_i,
    weight_j,
    weight_k,
    eigvec,
    eigvec_inv,
    block_inv_i,
    block_inv_j,
    band_i,
    band_j,
):
    nv = adjoint.shape[0]
    nj, ni = adjoint.shape[2], adjoint.shape[3]
    width = block_inv_i.shape[-1]
    state = adjoint.reshape(nv, nj, ni)
    src = source.reshape(nv, nj, ni)
    diag = diagonal.reshape(nv, nj, ni)
    wi = weight_i.reshape(1, nj, ni)
    wj = weight_j.reshape(1, nj, ni)
    wk = weight_k.reshape(1, nj, ni)

    first_i, last_i = inflow_terms(block_inv_i, band_i)
    first_j, last_j = inflow_terms(block_inv_j, band_j)

    blk = jax.ShapeDtypeStruct((nv, nj, ni), jnp.float32)
    ends_i = jax.ShapeDtypeStruct((lax.axis_size("ia"), 16, nj), jnp.float32)
    ends_j = jax.ShapeDtypeStruct((lax.axis_size("ja"), 16, ni), jnp.float32)
    face = jax.ShapeDtypeStruct((nv, ni), jnp.float32)
    scratch = [pltpu.VMEM((nv, nj, ni), jnp.float32)]
    res_call = _call(residual_kernel, 14, (12,), (blk, blk, ends_i), scratch)
    across_call = _call(across_i_kernel, 7, (0, 3), (blk, ends_j), [])
    update_call = _call(update_kernel, 8, (0, 4, 7), (blk, face, face, face, face), scratch)
    dinv_i_t = jnp.swapaxes(block_inv_i, 1, 2)
    step_i = carry_step(first_i, last_i).reshape(-1)
    step_j = carry_step(first_j, last_j).reshape(-1)
    me_i = lax.axis_index("ia").astype(jnp.int32).reshape(1)
    me_j = lax.axis_index("ja").astype(jnp.int32).reshape(1)

    residual = src
    faces = (state[:, :, ni - 1], state[:, :, 0], state[:, nj - 1, :], state[:, 0, :])
    for step in range(ITERS):
        lo_i = shifted(faces[0], "ia", 1)
        hi_i = shifted(faces[1], "ia", -1)
        lo_j = shifted(faces[2], "ja", 1)
        hi_j = shifted(faces[3], "ja", -1)
        lo_k = shifted(state, "ka", 1)
        hi_k = shifted(state, "ka", -1)
        residual, plain_i, ends_i = res_call(
            state, src, diag, wi[0], wj[0], wk[0], lo_i, hi_i, lo_j, hi_j, lo_k, hi_k, eigvec_inv, dinv_i_t
        )
        gathered_i = gather_ends(ends_i, "ia")
        plain_j, ends_j = across_call(me_i, plain_i, gathered_i, step_i, first_i, last_i, block_inv_j)
        gathered_j = gather_ends(ends_j, "ja")
        state, *faces = update_call(me_j, state, plain_j, gathered_j, step_j, first_j, last_j, eigvec)
    return (state.reshape(adjoint.shape), residual.reshape(adjoint.shape))


def solution(mesh):
    return jax.shard_map(
        local,
        mesh=mesh,
        in_specs=(
            P(None, "ka", "ja", "ia"),
            P(None, "ka", "ja", "ia"),
            P(None, "ka", "ja", "ia"),
            P("ka", "ja", "ia"),
            P("ka", "ja", "ia"),
            P("ka", "ja", "ia"),
            P(),
            P(),
            P(),
            P(),
            P(),
            P(),
        ),
        out_specs=(P(None, "ka", "ja", "ia"), P(None, "ka", "ja", "ia")),
        check_vma=False,
    )
```

```python
import jax
import jax.numpy as jnp
from jax import lax
from jax.experimental import pallas as pl
from jax.experimental.pallas import tpu as pltpu
from jax.sharding import PartitionSpec as P

ITERS = 2
HI = lax.Precision.HIGHEST


def shifted(value, axis, by):
    length = lax.axis_size(axis)
    pairs = [(i, i + by) for i in range(length) if 0 <= i + by < length]
    return lax.ppermute(value, axis, pairs)


def inflow_terms(dinv, band):
    coef_one = band[:, 0][:, None]
    coef_two = band[:, 1][:, None]
    resp_last = -(coef_one * dinv[:, :, 0] + coef_two * dinv[:, :, 1])
    resp_first = -coef_two * dinv[:, :, 0]
    return resp_first, resp_last


def carry_step(resp_first, resp_last):
    width = resp_first.shape[-1]
    top = jnp.stack([resp_first[:, width - 2], resp_last[:, width - 2]])
    bottom = jnp.stack([resp_first[:, width - 1], resp_last[:, width - 1]])
    return jnp.stack([top, bottom])


def gather_ends(copies, axis):
    return lax.all_to_all(copies, axis, 0, 0, tiled=True)


def _vmem():
    return pl.BlockSpec(memory_space=pltpu.VMEM)


def _smem():
    return pl.BlockSpec(memory_space=pltpu.SMEM)


def _mm(a, b):
    return jnp.dot(a, b, precision=HI, preferred_element_type=jnp.float32)


def _stack_rows(rows, height):
    row = lax.broadcasted_iota(jnp.int32, (height, rows[0].shape[-1]), 0)
    tile = jnp.zeros((height, rows[0].shape[-1]), jnp.float32)
    for k, r in enumerate(rows):
        tile = jnp.where(row == k, r, tile)
    return tile


def _emit_copies(ends_out, first_rows, last_rows):
    top = _stack_rows(first_rows, 8)
    bottom = _stack_rows(last_rows, 8)
    for c in range(ends_out.shape[0]):
        ends_out[c, 0:8, :] = top
        ends_out[c, 8:16, :] = bottom


def _coef(step, a, d, nv, n):
    row = lax.broadcasted_iota(jnp.int32, (8, n), 0)
    tile = jnp.zeros((8, n), jnp.float32)
    for v in range(nv):
        tile = jnp.where(row == v, step[(a * 2 + d) * nv + v], tile)
    return tile


def _mm_nt(a, b):
    return lax.dot_general(a, b, (((1,), (1,)), ((), ())), precision=HI, preferred_element_type=jnp.float32)


def _column(vec, shape):
    return jnp.transpose(jnp.broadcast_to(vec, (shape[1], shape[0])))


def residual_kernel(state, src, diag, wi, wj, wk, lo_i, hi_i, lo_j, hi_j, lo_k, hi_k, mix, dinv_t, tail,
                    res_out, plain_out, ends_out, chars):
    nv, nj, ni = state.shape
    lane = lax.broadcasted_iota(jnp.int32, (nj, ni), 1)
    row = lax.broadcasted_iota(jnp.int32, (nj, ni), 0)
    for v in range(nv):
        x = state[v]
        right_i = jnp.where(lane == ni - 1, _column(hi_i[v : v + 1, :], (nj, ni)), pltpu.roll(x, ni - 1, 1))
        left_i = jnp.where(lane == 0, _column(lo_i[v : v + 1, :], (nj, ni)), pltpu.roll(x, 1, 1))
        up_j = jnp.where(row == nj - 1, hi_j[v : v + 1, :], pltpu.roll(x, nj - 1, 0))
        down_j = jnp.where(row == 0, lo_j[v : v + 1, :], pltpu.roll(x, 1, 0))
        res_out[v] = (
            src[v]
            - diag[v] * x
            + wi[...] * (right_i + left_i)
            + wj[...] * (up_j + down_j)
            + wk[...] * (hi_k[v] + lo_k[v])
        )
    for u in range(nv):
        acc = mix[u, 0] * res_out[0]
        for v in range(1, nv):
            acc = acc + mix[u, v] * res_out[v]
        chars[u] = acc
    first_rows, last_rows = [], []
    for u in range(nv):
        plain_out[u] = _mm(chars[u], dinv_t[u])
        ends = _mm_nt(tail[u], chars[u])
        first_rows.append(ends[6:7, :])
        last_rows.append(ends[7:8, :])
    _emit_copies(ends_out, first_rows, last_rows)


def _inbound(gathered, step, me, nv):
    n = gathered.shape[-1]
    zero = jnp.zeros((8, n), jnp.float32)
    m00, m01 = _coef(step, 0, 0, nv, n), _coef(step, 0, 1, nv, n)
    m10, m11 = _coef(step, 1, 0, nv, n), _coef(step, 1, 1, nv, n)

    def body(c, carry):
        e0, e1 = carry
        n0 = m00 * e0 + m01 * e1 + gathered[c, 0:8, :]
        n1 = m10 * e0 + m11 * e1 + gathered[c, 8:16, :]
        return n0, n1

    return lax.fori_loop(0, me, body, (zero, zero))


def across_i_kernel(me, plain, gathered, step, first, last, dinv, out, ends_out):
    nv, nj, ni = plain.shape
    in_first, in_last = _inbound(gathered, step, me[0], nv)
    first_rows, last_rows = [], []
    for v in range(nv):
        fixed = (
            plain[v]
            + _column(in_first[v : v + 1, :], (nj, ni)) * first[v : v + 1, :]
            + _column(in_last[v : v + 1, :], (nj, ni)) * last[v : v + 1, :]
        )
        solved = _mm(dinv[v], fixed)
        out[v] = solved
        first_rows.append(solved[nj - 2 : nj - 1, :])
        last_rows.append(solved[nj - 1 : nj, :])
    _emit_copies(ends_out, first_rows, last_rows)


def update_kernel(me, state, plain, gathered, step, first, last, mix, pick, out, lo_i, hi_i, lo_j, hi_j, chars):
    nv, nj, ni = plain.shape
    in_first, in_last = _inbound(gathered, step, me[0], nv)
    for v in range(nv):
        chars[v] = plain[v] + in_first[v : v + 1, :] * first[v] + in_last[v : v + 1, :] * last[v]
    for u in range(nv):
        total = mix[u, 0] * chars[0]
        for v in range(1, nv):
            total = total + mix[u, v] * chars[v]
        new = state[u] + total
        out[u] = new
        sides = _mm_nt(pick[...], new)
        lo_i[u : u + 1, :] = sides[1:2, :]
        hi_i[u : u + 1, :] = sides[0:1, :]
        lo_j[u : u + 1, :] = new[nj - 1 : nj, :]
        hi_j[u : u + 1, :] = new[0:1, :]


def _call(kernel, n_in, smem_at, outs, scratch):
    specs = [_smem() if k in smem_at else _vmem() for k in range(n_in)]
    return pl.pallas_call(
        kernel,
        out_shape=outs,
        in_specs=specs,
        out_specs=tuple(_vmem() for _ in outs) if isinstance(outs, tuple) else _vmem(),
        scratch_shapes=scratch,
    )


def local(
    adjoint,
    source,
    diagonal,
    weight_i,
    weight_j,
    weight_k,
    eigvec,
    eigvec_inv,
    block_inv_i,
    block_inv_j,
    band_i,
    band_j,
):
    nv = adjoint.shape[0]
    nj, ni = adjoint.shape[2], adjoint.shape[3]
    width = block_inv_i.shape[-1]
    state = adjoint.reshape(nv, nj, ni)
    src = source.reshape(nv, nj, ni)
    diag = diagonal.reshape(nv, nj, ni)
    wi = weight_i.reshape(1, nj, ni)
    wj = weight_j.reshape(1, nj, ni)
    wk = weight_k.reshape(1, nj, ni)

    first_i, last_i = inflow_terms(block_inv_i, band_i)
    first_j, last_j = inflow_terms(block_inv_j, band_j)

    blk = jax.ShapeDtypeStruct((nv, nj, ni), jnp.float32)
    ends_i = jax.ShapeDtypeStruct((lax.axis_size("ia"), 16, nj), jnp.float32)
    ends_j = jax.ShapeDtypeStruct((lax.axis_size("ja"), 16, ni), jnp.float32)
    face = jax.ShapeDtypeStruct((nv, ni), jnp.float32)
    scratch = [pltpu.VMEM((nv, nj, ni), jnp.float32)]
    res_call = _call(residual_kernel, 15, (12,), (blk, blk, ends_i), scratch)
    across_call = _call(across_i_kernel, 7, (0, 3), (blk, ends_j), [])
    update_call = _call(update_kernel, 9, (0, 4, 7), (blk, face, face, face, face), scratch)
    tail_i = block_inv_i[:, ni - 8 :, :]
    first_j_cols = jnp.broadcast_to(first_j[:, :, None], (nv, nj, ni))
    last_j_cols = jnp.broadcast_to(last_j[:, :, None], (nv, nj, ni))
    lane8 = lax.broadcasted_iota(jnp.int32, (8, ni), 1)
    row8 = lax.broadcasted_iota(jnp.int32, (8, ni), 0)
    pick = ((row8 == 0) & (lane8 == 0)) | ((row8 == 1) & (lane8 == ni - 1))
    pick = pick.astype(jnp.float32)
    dinv_i_t = jnp.swapaxes(block_inv_i, 1, 2)
    step_i = carry_step(first_i, last_i).reshape(-1)
    step_j = carry_step(first_j, last_j).reshape(-1)
    me_i = lax.axis_index("ia").astype(jnp.int32).reshape(1)
    me_j = lax.axis_index("ja").astype(jnp.int32).reshape(1)

    residual = src
    faces = (state[:, :, ni - 1], state[:, :, 0], state[:, nj - 1, :], state[:, 0, :])
    for step in range(ITERS):
        lo_i = shifted(faces[0], "ia", 1)
        hi_i = shifted(faces[1], "ia", -1)
        lo_j = shifted(faces[2], "ja", 1)
        hi_j = shifted(faces[3], "ja", -1)
        lo_k = shifted(state, "ka", 1)
        hi_k = shifted(state, "ka", -1)
        residual, plain_i, ends_i = res_call(
            state, src, diag, wi[0], wj[0], wk[0], lo_i, hi_i, lo_j, hi_j, lo_k, hi_k, eigvec_inv, dinv_i_t, tail_i
        )
        gathered_i = gather_ends(ends_i, "ia")
        plain_j, ends_j = across_call(me_i, plain_i, gathered_i, step_i, first_i, last_i, block_inv_j)
        gathered_j = gather_ends(ends_j, "ja")
        state, *faces = update_call(
            me_j, state, plain_j, gathered_j, step_j, first_j_cols, last_j_cols, eigvec, pick
        )
    return (state.reshape(adjoint.shape), residual.reshape(adjoint.shape))


def solution(mesh):
    return jax.shard_map(
        local,
        mesh=mesh,
        in_specs=(
            P(None, "ka", "ja", "ia"),
            P(None, "ka", "ja", "ia"),
            P(None, "ka", "ja", "ia"),
            P("ka", "ja", "ia"),
            P("ka", "ja", "ia"),
            P("ka", "ja", "ia"),
            P(),
            P(),
            P(),
            P(),
            P(),
            P(),
        ),
        out_specs=(P(None, "ka", "ja", "ia"), P(None, "ka", "ja", "ia")),
        check_vma=False,
    )
```

```python
import jax
import jax.numpy as jnp
from jax import lax
from jax.experimental import pallas as pl
from jax.experimental.pallas import tpu as pltpu
from jax.sharding import PartitionSpec as P

ITERS = 2
HI = lax.Precision.HIGHEST


def shifted(value, axis, by):
    length = lax.axis_size(axis)
    pairs = [(i, i + by) for i in range(length) if 0 <= i + by < length]
    return lax.ppermute(value, axis, pairs)


def inflow_terms(dinv, band):
    coef_one = band[:, 0][:, None]
    coef_two = band[:, 1][:, None]
    resp_last = -(coef_one * dinv[:, :, 0] + coef_two * dinv[:, :, 1])
    resp_first = -coef_two * dinv[:, :, 0]
    return resp_first, resp_last


def carry_step(resp_first, resp_last):
    width = resp_first.shape[-1]
    top = jnp.stack([resp_first[:, width - 2], resp_last[:, width - 2]])
    bottom = jnp.stack([resp_first[:, width - 1], resp_last[:, width - 1]])
    return jnp.stack([top, bottom])


def gather_ends(copies, axis):
    return lax.all_to_all(copies, axis, 0, 0, tiled=True)


def _vmem():
    return pl.BlockSpec(memory_space=pltpu.VMEM)


def _smem():
    return pl.BlockSpec(memory_space=pltpu.SMEM)


def _mm(a, b):
    return jnp.dot(a, b, precision=lax.Precision.HIGH, preferred_element_type=jnp.float32)


def _stack_rows(rows, height):
    row = lax.broadcasted_iota(jnp.int32, (height, rows[0].shape[-1]), 0)
    tile = jnp.zeros((height, rows[0].shape[-1]), jnp.float32)
    for k, r in enumerate(rows):
        tile = jnp.where(row == k, r, tile)
    return tile


def _emit_copies(ends_out, first_rows, last_rows):
    top = _stack_rows(first_rows, 8)
    bottom = _stack_rows(last_rows, 8)
    for c in range(ends_out.shape[0]):
        ends_out[c, 0:8, :] = top
        ends_out[c, 8:16, :] = bottom


def _coef(step, a, d, nv, n):
    row = lax.broadcasted_iota(jnp.int32, (8, n), 0)
    tile = jnp.zeros((8, n), jnp.float32)
    for v in range(nv):
        tile = jnp.where(row == v, step[(a * 2 + d) * nv + v], tile)
    return tile


def _column(vec, shape):
    return jnp.transpose(jnp.broadcast_to(vec, (shape[1], shape[0])))


def residual_kernel(state, src, diag, wi, wj, wk, lo_i, hi_i, lo_j, hi_j, lo_k, hi_k, mix, dinv_t,
                    res_out, plain_out, ends_out, chars):
    nv, nj, ni = state.shape
    lane = lax.broadcasted_iota(jnp.int32, (nj, ni), 1)
    row = lax.broadcasted_iota(jnp.int32, (nj, ni), 0)
    for v in range(nv):
        x = state[v]
        right_i = jnp.where(lane == ni - 1, _column(hi_i[v : v + 1, :], (nj, ni)), pltpu.roll(x, ni - 1, 1))
        left_i = jnp.where(lane == 0, _column(lo_i[v : v + 1, :], (nj, ni)), pltpu.roll(x, 1, 1))
        up_j = jnp.where(row == nj - 1, hi_j[v : v + 1, :], pltpu.roll(x, nj - 1, 0))
        down_j = jnp.where(row == 0, lo_j[v : v + 1, :], pltpu.roll(x, 1, 0))
        res_out[v] = (
            src[v]
            - diag[v] * x
            + wi[...] * (right_i + left_i)
            + wj[...] * (up_j + down_j)
            + wk[...] * (hi_k[v] + lo_k[v])
        )
    for u in range(nv):
        acc = mix[u, 0] * res_out[0]
        for v in range(1, nv):
            acc = acc + mix[u, v] * res_out[v]
        chars[u] = acc
    first_rows, last_rows = [], []
    for u in range(nv):
        plain = _mm(chars[u], dinv_t[u])
        plain_out[u] = plain
        turned = jnp.transpose(plain)
        first_rows.append(turned[ni - 2 : ni - 1, :])
        last_rows.append(turned[ni - 1 : ni, :])
    _emit_copies(ends_out, first_rows, last_rows)


def _inbound(gathered, step, me, nv):
    n = gathered.shape[-1]
    zero = jnp.zeros((8, n), jnp.float32)
    m00, m01 = _coef(step, 0, 0, nv, n), _coef(step, 0, 1, nv, n)
    m10, m11 = _coef(step, 1, 0, nv, n), _coef(step, 1, 1, nv, n)

    def body(c, carry):
        e0, e1 = carry
        n0 = m00 * e0 + m01 * e1 + gathered[c, 0:8, :]
        n1 = m10 * e0 + m11 * e1 + gathered[c, 8:16, :]
        return n0, n1

    return lax.fori_loop(0, me, body, (zero, zero))


def across_i_kernel(me, plain, gathered, step, first, last, dinv, out, ends_out):
    nv, nj, ni = plain.shape
    in_first, in_last = _inbound(gathered, step, me[0], nv)
    first_rows, last_rows = [], []
    for v in range(nv):
        fixed = (
            plain[v]
            + _column(in_first[v : v + 1, :], (nj, ni)) * first[v : v + 1, :]
            + _column(in_last[v : v + 1, :], (nj, ni)) * last[v : v + 1, :]
        )
        solved = _mm(dinv[v], fixed)
        out[v] = solved
        first_rows.append(solved[nj - 2 : nj - 1, :])
        last_rows.append(solved[nj - 1 : nj, :])
    _emit_copies(ends_out, first_rows, last_rows)


def update_kernel(me, state, plain, gathered, step, first, last, mix, out, lo_i, hi_i, lo_j, hi_j, chars):
    nv, nj, ni = plain.shape
    in_first, in_last = _inbound(gathered, step, me[0], nv)
    for v in range(nv):
        chars[v] = (
            plain[v]
            + in_first[v : v + 1, :] * _column(first[v : v + 1, :], (nj, ni))
            + in_last[v : v + 1, :] * _column(last[v : v + 1, :], (nj, ni))
        )
    for u in range(nv):
        total = mix[u, 0] * chars[0]
        for v in range(1, nv):
            total = total + mix[u, v] * chars[v]
        new = state[u] + total
        out[u] = new
        turned = jnp.transpose(new)
        lo_i[u : u + 1, :] = turned[ni - 1 : ni, :]
        hi_i[u : u + 1, :] = turned[0:1, :]
        lo_j[u : u + 1, :] = new[nj - 1 : nj, :]
        hi_j[u : u + 1, :] = new[0:1, :]


def _call(kernel, n_in, smem_at, outs, scratch):
    specs = [_smem() if k in smem_at else _vmem() for k in range(n_in)]
    return pl.pallas_call(
        kernel,
        out_shape=outs,
        in_specs=specs,
        out_specs=tuple(_vmem() for _ in outs) if isinstance(outs, tuple) else _vmem(),
        scratch_shapes=scratch,
    )


def local(
    adjoint,
    source,
    diagonal,
    weight_i,
    weight_j,
    weight_k,
    eigvec,
    eigvec_inv,
    block_inv_i,
    block_inv_j,
    band_i,
    band_j,
):
    nv = adjoint.shape[0]
    nj, ni = adjoint.shape[2], adjoint.shape[3]
    width = block_inv_i.shape[-1]
    state = adjoint.reshape(nv, nj, ni)
    src = source.reshape(nv, nj, ni)
    diag = diagonal.reshape(nv, nj, ni)
    wi = weight_i.reshape(1, nj, ni)
    wj = weight_j.reshape(1, nj, ni)
    wk = weight_k.reshape(1, nj, ni)

    first_i, last_i = inflow_terms(block_inv_i, band_i)
    first_j, last_j = inflow_terms(block_inv_j, band_j)

    blk = jax.ShapeDtypeStruct((nv, nj, ni), jnp.float32)
    ends_i = jax.ShapeDtypeStruct((lax.axis_size("ia"), 16, nj), jnp.float32)
    ends_j = jax.ShapeDtypeStruct((lax.axis_size("ja"), 16, ni), jnp.float32)
    face = jax.ShapeDtypeStruct((nv, ni), jnp.float32)
    scratch = [pltpu.VMEM((nv, nj, ni), jnp.float32)]
    res_call = _call(residual_kernel, 14, (12,), (blk, blk, ends_i), scratch)
    across_call = _call(across_i_kernel, 7, (0, 3), (blk, ends_j), [])
    update_call = _call(update_kernel, 8, (0, 4, 7), (blk, face, face, face, face), scratch)
    dinv_i_t = jnp.swapaxes(block_inv_i, 1, 2)
    step_i = carry_step(first_i, last_i).reshape(-1)
    step_j = carry_step(first_j, last_j).reshape(-1)
    me_i = lax.axis_index("ia").astype(jnp.int32).reshape(1)
    me_j = lax.axis_index("ja").astype(jnp.int32).reshape(1)

    residual = src
    faces = (state[:, :, ni - 1], state[:, :, 0], state[:, nj - 1, :], state[:, 0, :])
    for step in range(ITERS):
        lo_i = shifted(faces[0], "ia", 1)
        hi_i = shifted(faces[1], "ia", -1)
        lo_j = shifted(faces[2], "ja", 1)
        hi_j = shifted(faces[3], "ja", -1)
        lo_k = shifted(state, "ka", 1)
        hi_k = shifted(state, "ka", -1)
        residual, plain_i, ends_i = res_call(
            state, src, diag, wi[0], wj[0], wk[0], lo_i, hi_i, lo_j, hi_j, lo_k, hi_k, eigvec_inv, dinv_i_t
        )
        gathered_i = gather_ends(ends_i, "ia")
        plain_j, ends_j = across_call(me_i, plain_i, gathered_i, step_i, first_i, last_i, block_inv_j)
        gathered_j = gather_ends(ends_j, "ja")
        state, *faces = update_call(me_j, state, plain_j, gathered_j, step_j, first_j, last_j, eigvec)
    return (state.reshape(adjoint.shape), residual.reshape(adjoint.shape))


def solution(mesh):
    return jax.shard_map(
        local,
        mesh=mesh,
        in_specs=(
            P(None, "ka", "ja", "ia"),
            P(None, "ka", "ja", "ia"),
            P(None, "ka", "ja", "ia"),
            P("ka", "ja", "ia"),
            P("ka", "ja", "ia"),
            P("ka", "ja", "ia"),
            P(),
            P(),
            P(),
            P(),
            P(),
            P(),
        ),
        out_specs=(P(None, "ka", "ja", "ia"), P(None, "ka", "ja", "ia")),
        check_vma=False,
    )
```

```python
import jax
import jax.numpy as jnp
from jax import lax
from jax.experimental import pallas as pl
from jax.experimental.pallas import tpu as pltpu
from jax.sharding import PartitionSpec as P

ITERS = 2
HI = lax.Precision.HIGHEST


def shifted(value, axis, by):
    length = lax.axis_size(axis)
    pairs = [(i, i + by) for i in range(length) if 0 <= i + by < length]
    return lax.ppermute(value, axis, pairs)


def inflow_terms(dinv, band):
    coef_one = band[:, 0][:, None]
    coef_two = band[:, 1][:, None]
    resp_last = -(coef_one * dinv[:, :, 0] + coef_two * dinv[:, :, 1])
    resp_first = -coef_two * dinv[:, :, 0]
    return resp_first, resp_last


def carry_step(resp_first, resp_last):
    width = resp_first.shape[-1]
    top = jnp.stack([resp_first[:, width - 2], resp_last[:, width - 2]])
    bottom = jnp.stack([resp_first[:, width - 1], resp_last[:, width - 1]])
    return jnp.stack([top, bottom])


def gather_ends(copies, axis):
    return lax.all_to_all(copies, axis, 0, 0, tiled=True)


def _vmem():
    return pl.BlockSpec(memory_space=pltpu.VMEM)


def _smem():
    return pl.BlockSpec(memory_space=pltpu.SMEM)


def _mm(a, b):
    return jnp.dot(a, b, precision=HI, preferred_element_type=jnp.float32)


def _stack_rows(rows, height):
    row = lax.broadcasted_iota(jnp.int32, (height, rows[0].shape[-1]), 0)
    tile = jnp.zeros((height, rows[0].shape[-1]), jnp.float32)
    for k, r in enumerate(rows):
        tile = jnp.where(row == k, r, tile)
    return tile


def _emit_copies(ends_out, first_rows, last_rows):
    top = _stack_rows(first_rows, 8)
    bottom = _stack_rows(last_rows, 8)
    for c in range(ends_out.shape[0]):
        ends_out[c, 0:8, :] = top
        ends_out[c, 8:16, :] = bottom


def _coef(step, a, d, nv, n):
    row = lax.broadcasted_iota(jnp.int32, (8, n), 0)
    tile = jnp.zeros((8, n), jnp.float32)
    for v in range(nv):
        tile = jnp.where(row == v, step[(a * 2 + d) * nv + v], tile)
    return tile


def _column(vec, shape):
    return jnp.transpose(jnp.broadcast_to(vec, (shape[1], shape[0])))


def residual_kernel(state, src, diag, wi, wj, wk, lo_i, hi_i, lo_j, hi_j, lo_k, hi_k, mix, dinv_t, *rest):
    if len(rest) == 4:
        res_out, plain_out, ends_out, chars = rest
        near_k = None
    else:
        inflow_k, first_j, last_j, back, res_out, plain_out, ends_out, chars = rest
        near_k = _neighbour_update(inflow_k, first_j, last_j, back, state.shape)
    nv, nj, ni = state.shape
    lane = lax.broadcasted_iota(jnp.int32, (nj, ni), 1)
    row = lax.broadcasted_iota(jnp.int32, (nj, ni), 0)
    for v in range(nv):
        x = state[v]
        right_i = jnp.where(lane == ni - 1, _column(hi_i[v : v + 1, :], (nj, ni)), pltpu.roll(x, ni - 1, 1))
        left_i = jnp.where(lane == 0, _column(lo_i[v : v + 1, :], (nj, ni)), pltpu.roll(x, 1, 1))
        up_j = jnp.where(row == nj - 1, hi_j[v : v + 1, :], pltpu.roll(x, nj - 1, 0))
        down_j = jnp.where(row == 0, lo_j[v : v + 1, :], pltpu.roll(x, 1, 0))
        res_out[v] = (
            src[v]
            - diag[v] * x
            + wi[...] * (right_i + left_i)
            + wj[...] * (up_j + down_j)
            + wk[...] * (hi_k[v] + lo_k[v] if near_k is None else hi_k[v] + lo_k[v] + near_k[v])
        )
    for u in range(nv):
        acc = mix[u, 0] * res_out[0]
        for v in range(1, nv):
            acc = acc + mix[u, v] * res_out[v]
        chars[u] = acc
    first_rows, last_rows = [], []
    for u in range(nv):
        plain = _mm(chars[u], dinv_t[u])
        plain_out[u] = plain
        turned = jnp.transpose(plain)
        first_rows.append(turned[ni - 2 : ni - 1, :])
        last_rows.append(turned[ni - 1 : ni, :])
    _emit_copies(ends_out, first_rows, last_rows)


def _neighbour_update(inflow_k, first_j, last_j, back, shape):
    nv, nj, ni = shape
    cols_f = [_column(first_j[v : v + 1, :], (nj, ni)) for v in range(nv)]
    cols_l = [_column(last_j[v : v + 1, :], (nj, ni)) for v in range(nv)]
    near = []
    for u in range(nv):
        acc = None
        for v in range(nv):
            term = (back[u, v] * inflow_k[v : v + 1, :]) * cols_f[v] + (back[u, v] * inflow_k[8 + v : 9 + v, :]) * cols_l[v]
            acc = term if acc is None else acc + term
        near.append(acc)
    return near


def _inbound(gathered, step, me, nv):
    n = gathered.shape[-1]
    zero = jnp.zeros((8, n), jnp.float32)
    m00, m01 = _coef(step, 0, 0, nv, n), _coef(step, 0, 1, nv, n)
    m10, m11 = _coef(step, 1, 0, nv, n), _coef(step, 1, 1, nv, n)

    def body(c, carry):
        e0, e1 = carry
        n0 = m00 * e0 + m01 * e1 + gathered[c, 0:8, :]
        n1 = m10 * e0 + m11 * e1 + gathered[c, 8:16, :]
        return n0, n1

    return lax.fori_loop(0, me, body, (zero, zero))


def across_i_kernel(me, plain, gathered, step, first, last, dinv, state, back, out, ends_out, partial):
    nv, nj, ni = plain.shape
    in_first, in_last = _inbound(gathered, step, me[0], nv)
    first_rows, last_rows = [], []
    for v in range(nv):
        fixed = (
            plain[v]
            + _column(in_first[v : v + 1, :], (nj, ni)) * first[v : v + 1, :]
            + _column(in_last[v : v + 1, :], (nj, ni)) * last[v : v + 1, :]
        )
        solved = _mm(dinv[v], fixed)
        out[v] = solved
        first_rows.append(solved[nj - 2 : nj - 1, :])
        last_rows.append(solved[nj - 1 : nj, :])
    _emit_copies(ends_out, first_rows, last_rows)
    for u in range(nv):
        total = back[u, 0] * out[0]
        for v in range(1, nv):
            total = total + back[u, v] * out[v]
        partial[u] = state[u] + total


def update_kernel(me, state, plain, gathered, step, first, last, mix, out, lo_i, hi_i, lo_j, hi_j, inflow, chars):
    nv, nj, ni = plain.shape
    in_first, in_last = _inbound(gathered, step, me[0], nv)
    inflow[0:8, :] = in_first
    inflow[8:16, :] = in_last
    for v in range(nv):
        chars[v] = (
            plain[v]
            + in_first[v : v + 1, :] * _column(first[v : v + 1, :], (nj, ni))
            + in_last[v : v + 1, :] * _column(last[v : v + 1, :], (nj, ni))
        )
    for u in range(nv):
        total = mix[u, 0] * chars[0]
        for v in range(1, nv):
            total = total + mix[u, v] * chars[v]
        new = state[u] + total
        out[u] = new
        turned = jnp.transpose(new)
        lo_i[u : u + 1, :] = turned[ni - 1 : ni, :]
        hi_i[u : u + 1, :] = turned[0:1, :]
        lo_j[u : u + 1, :] = new[nj - 1 : nj, :]
        hi_j[u : u + 1, :] = new[0:1, :]


def _call(kernel, n_in, smem_at, outs, scratch):
    specs = [_smem() if k in smem_at else _vmem() for k in range(n_in)]
    return pl.pallas_call(
        kernel,
        out_shape=outs,
        in_specs=specs,
        out_specs=tuple(_vmem() for _ in outs) if isinstance(outs, tuple) else _vmem(),
        scratch_shapes=scratch,
    )


def local(
    adjoint,
    source,
    diagonal,
    weight_i,
    weight_j,
    weight_k,
    eigvec,
    eigvec_inv,
    block_inv_i,
    block_inv_j,
    band_i,
    band_j,
):
    nv = adjoint.shape[0]
    nj, ni = adjoint.shape[2], adjoint.shape[3]
    width = block_inv_i.shape[-1]
    state = adjoint.reshape(nv, nj, ni)
    src = source.reshape(nv, nj, ni)
    diag = diagonal.reshape(nv, nj, ni)
    wi = weight_i.reshape(1, nj, ni)
    wj = weight_j.reshape(1, nj, ni)
    wk = weight_k.reshape(1, nj, ni)

    first_i, last_i = inflow_terms(block_inv_i, band_i)
    first_j, last_j = inflow_terms(block_inv_j, band_j)

    blk = jax.ShapeDtypeStruct((nv, nj, ni), jnp.float32)
    ends_i = jax.ShapeDtypeStruct((lax.axis_size("ia"), 16, nj), jnp.float32)
    ends_j = jax.ShapeDtypeStruct((lax.axis_size("ja"), 16, ni), jnp.float32)
    face = jax.ShapeDtypeStruct((nv, ni), jnp.float32)
    scratch = [pltpu.VMEM((nv, nj, ni), jnp.float32)]
    res_call = _call(residual_kernel, 14, (12,), (blk, blk, ends_i), scratch)
    res_next_call = _call(residual_kernel, 18, (12, 17), (blk, blk, ends_i), scratch)
    across_call = _call(across_i_kernel, 9, (0, 3, 8), (blk, ends_j, blk), [])
    inflow = jax.ShapeDtypeStruct((16, ni), jnp.float32)
    update_call = _call(update_kernel, 8, (0, 4, 7), (blk, face, face, face, face, inflow), scratch)
    dinv_i_t = jnp.swapaxes(block_inv_i, 1, 2)
    step_i = carry_step(first_i, last_i).reshape(-1)
    step_j = carry_step(first_j, last_j).reshape(-1)
    me_i = lax.axis_index("ia").astype(jnp.int32).reshape(1)
    me_j = lax.axis_index("ja").astype(jnp.int32).reshape(1)

    residual = src
    faces = (state[:, :, ni - 1], state[:, :, 0], state[:, nj - 1, :], state[:, 0, :])
    lo_k = shifted(state, "ka", 1)
    hi_k = shifted(state, "ka", -1)
    inflow_k = None
    for step in range(ITERS):
        lo_i = shifted(faces[0], "ia", 1)
        hi_i = shifted(faces[1], "ia", -1)
        lo_j = shifted(faces[2], "ja", 1)
        hi_j = shifted(faces[3], "ja", -1)
        common = (state, src, diag, wi[0], wj[0], wk[0], lo_i, hi_i, lo_j, hi_j, lo_k, hi_k, eigvec_inv, dinv_i_t)
        if inflow_k is None:
            residual, plain_i, ends_i = res_call(*common)
        else:
            residual, plain_i, ends_i = res_next_call(*common, inflow_k, first_j, last_j, eigvec)
        gathered_i = gather_ends(ends_i, "ia")
        plain_j, ends_j, partial = across_call(
            me_i, plain_i, gathered_i, step_i, first_i, last_i, block_inv_j, state, eigvec
        )
        if step + 1 < ITERS:
            lo_k = shifted(partial, "ka", 1)
            hi_k = shifted(partial, "ka", -1)
        gathered_j = gather_ends(ends_j, "ja")
        state, *faces, inflow_out = update_call(me_j, state, plain_j, gathered_j, step_j, first_j, last_j, eigvec)
        if step + 1 < ITERS:
            inflow_k = shifted(inflow_out, "ka", 1) + shifted(inflow_out, "ka", -1)
    return (state.reshape(adjoint.shape), residual.reshape(adjoint.shape))


def solution(mesh):
    return jax.shard_map(
        local,
        mesh=mesh,
        in_specs=(
            P(None, "ka", "ja", "ia"),
            P(None, "ka", "ja", "ia"),
            P(None, "ka", "ja", "ia"),
            P("ka", "ja", "ia"),
            P("ka", "ja", "ia"),
            P("ka", "ja", "ia"),
            P(),
            P(),
            P(),
            P(),
            P(),
            P(),
        ),
        out_specs=(P(None, "ka", "ja", "ia"), P(None, "ka", "ja", "ia")),
        check_vma=False,
    )
```

```python
import jax
import jax.numpy as jnp
from jax import lax
from jax.experimental import pallas as pl
from jax.experimental.pallas import tpu as pltpu
from jax.sharding import PartitionSpec as P

ITERS = 2
HI = lax.Precision.HIGHEST


def shifted(value, axis, by):
    length = lax.axis_size(axis)
    pairs = [(i, i + by) for i in range(length) if 0 <= i + by < length]
    return lax.ppermute(value, axis, pairs)


def inflow_terms(dinv, band):
    coef_one = band[:, 0][:, None]
    coef_two = band[:, 1][:, None]
    resp_last = -(coef_one * dinv[:, :, 0] + coef_two * dinv[:, :, 1])
    resp_first = -coef_two * dinv[:, :, 0]
    return resp_first, resp_last


def carry_step(resp_first, resp_last):
    width = resp_first.shape[-1]
    top = jnp.stack([resp_first[:, width - 2], resp_last[:, width - 2]])
    bottom = jnp.stack([resp_first[:, width - 1], resp_last[:, width - 1]])
    return jnp.stack([top, bottom])


def gather_ends(copies, axis):
    return lax.all_to_all(copies, axis, 0, 0, tiled=True)


def _vmem():
    return pl.BlockSpec(memory_space=pltpu.VMEM)


def _smem():
    return pl.BlockSpec(memory_space=pltpu.SMEM)


def _mm(a, b):
    return jnp.dot(a, b, precision=HI, preferred_element_type=jnp.float32)


def _stack_rows(rows, height):
    row = lax.broadcasted_iota(jnp.int32, (height, rows[0].shape[-1]), 0)
    tile = jnp.zeros((height, rows[0].shape[-1]), jnp.float32)
    for k, r in enumerate(rows):
        tile = jnp.where(row == k, r, tile)
    return tile


def _emit_copies(ends_out, first_rows, last_rows):
    top = _stack_rows(first_rows, 8)
    bottom = _stack_rows(last_rows, 8)
    for c in range(ends_out.shape[0]):
        ends_out[c, 0:8, :] = top
        ends_out[c, 8:16, :] = bottom


def _coef(step, a, d, nv, n):
    row = lax.broadcasted_iota(jnp.int32, (8, n), 0)
    tile = jnp.zeros((8, n), jnp.float32)
    for v in range(nv):
        tile = jnp.where(row == v, step[(a * 2 + d) * nv + v], tile)
    return tile


def _column(vec, shape):
    return jnp.transpose(jnp.broadcast_to(vec, (shape[1], shape[0])))


def residual_kernel(state, src, diag, wi, wj, wk, lo_i, hi_i, lo_j, hi_j, lo_k, hi_k, mix, dinv_t,
                    res_out, plain_out, ends_out, chars):
    nv, nj, ni = state.shape
    lane = lax.broadcasted_iota(jnp.int32, (nj, ni), 1)
    row = lax.broadcasted_iota(jnp.int32, (nj, ni), 0)
    for v in range(nv):
        x = state[v]
        right_i = jnp.where(lane == ni - 1, _column(hi_i[v : v + 1, :], (nj, ni)), pltpu.roll(x, ni - 1, 1))
        left_i = jnp.where(lane == 0, _column(lo_i[v : v + 1, :], (nj, ni)), pltpu.roll(x, 1, 1))
        up_j = jnp.where(row == nj - 1, hi_j[v : v + 1, :], pltpu.roll(x, nj - 1, 0))
        down_j = jnp.where(row == 0, lo_j[v : v + 1, :], pltpu.roll(x, 1, 0))
        res_out[v] = (
            src[v]
            - diag[v] * x
            + wi[...] * (right_i + left_i)
            + wj[...] * (up_j + down_j)
            + wk[...] * (hi_k[v] + lo_k[v])
        )
    for u in range(nv):
        acc = mix[u, 0] * res_out[0]
        for v in range(1, nv):
            acc = acc + mix[u, v] * res_out[v]
        chars[u] = acc
    first_rows, last_rows = [], []
    for u in range(nv):
        plain = _mm(chars[u], dinv_t[u])
        plain_out[u] = plain
        turned = jnp.transpose(plain)
        first_rows.append(turned[ni - 2 : ni - 1, :])
        last_rows.append(turned[ni - 1 : ni, :])
    _emit_copies(ends_out, first_rows, last_rows)


def _inbound(gathered, step, me, nv):
    n = gathered.shape[-1]
    zero = jnp.zeros((8, n), jnp.float32)
    m00, m01 = _coef(step, 0, 0, nv, n), _coef(step, 0, 1, nv, n)
    m10, m11 = _coef(step, 1, 0, nv, n), _coef(step, 1, 1, nv, n)

    def body(c, carry):
        e0, e1 = carry
        n0 = m00 * e0 + m01 * e1 + gathered[c, 0:8, :]
        n1 = m10 * e0 + m11 * e1 + gathered[c, 8:16, :]
        return n0, n1

    return lax.fori_loop(0, me, body, (zero, zero))


def _around(gathered, step, me, nv):
    count, n = gathered.shape[0], gathered.shape[-1]
    zero = jnp.zeros((8, n), jnp.float32)
    m00, m01 = _coef(step, 0, 0, nv, n), _coef(step, 0, 1, nv, n)
    m10, m11 = _coef(step, 1, 0, nv, n), _coef(step, 1, 1, nv, n)

    def advance(e0, e1, c):
        return m00 * e0 + m01 * e1 + gathered[c, 0:8, :], m10 * e0 + m11 * e1 + gathered[c, 8:16, :]

    prev0, prev1 = lax.fori_loop(0, jnp.maximum(me - 1, 0), lambda c, e: advance(e[0], e[1], c), (zero, zero))
    stepped = advance(prev0, prev1, jnp.maximum(me - 1, 0))
    mine0 = jnp.where(me >= 1, stepped[0], zero)
    mine1 = jnp.where(me >= 1, stepped[1], zero)
    next0, next1 = advance(mine0, mine1, me)
    return (prev0, prev1), (mine0, mine1), (next0, next1)


def across_i_kernel(me, plain, gathered, step, first, last, dinv, state, back, out, ends_out):
    nv, nj, ni = plain.shape
    in_first, in_last = _inbound(gathered, step, me[0], nv)
    first_rows, last_rows = [], []
    for v in range(nv):
        fixed = (
            plain[v]
            + _column(in_first[v : v + 1, :], (nj, ni)) * first[v : v + 1, :]
            + _column(in_last[v : v + 1, :], (nj, ni)) * last[v : v + 1, :]
        )
        solved = _mm(dinv[v], fixed)
        out[v] = solved
        first_rows.append(solved[nj - 2 : nj - 1, :])
        last_rows.append(solved[nj - 1 : nj, :])
    _emit_copies(ends_out, first_rows, last_rows)
    bottom_rows, top_rows = [], []
    for u in range(nv):
        low = state[u, 0:1, :]
        high = state[u, nj - 1 : nj, :]
        for v in range(nv):
            low = low + back[u, v] * out[v, 0:1, :]
            high = high + back[u, v] * out[v, nj - 1 : nj, :]
        bottom_rows.append(low)
        top_rows.append(high)
    low_tile = _stack_rows(bottom_rows, 8)
    high_tile = _stack_rows(top_rows, 8)
    for c in range(ends_out.shape[0]):
        ends_out[c, 16:24, :] = low_tile
        ends_out[c, 24:32, :] = high_tile


def update_kernel(me, state, plain, gathered, step, first, last, mix, out, lo_i, hi_i, lo_j, hi_j, chars):
    nv, nj, ni = plain.shape
    count = gathered.shape[0]
    here = me[0]
    prev, (in_first, in_last), nxt = _around(gathered, step, here, nv)
    below = gathered[jnp.maximum(here - 1, 0), 24:32, :]
    above = gathered[jnp.minimum(here + 1, count - 1), 16:24, :]
    for u in range(nv):
        low = below[u : u + 1, :]
        high = above[u : u + 1, :]
        for v in range(nv):
            low = low + mix[u, v] * (
                prev[0][v : v + 1, :] * first[v : v + 1, nj - 1 : nj] + prev[1][v : v + 1, :] * last[v : v + 1, nj - 1 : nj]
            )
            high = high + mix[u, v] * (
                nxt[0][v : v + 1, :] * first[v : v + 1, 0:1] + nxt[1][v : v + 1, :] * last[v : v + 1, 0:1]
            )
        lo_j[u : u + 1, :] = jnp.where(here >= 1, low, 0.0)
        hi_j[u : u + 1, :] = jnp.where(here + 1 < count, high, 0.0)
    for v in range(nv):
        chars[v] = (
            plain[v]
            + in_first[v : v + 1, :] * _column(first[v : v + 1, :], (nj, ni))
            + in_last[v : v + 1, :] * _column(last[v : v + 1, :], (nj, ni))
        )
    for u in range(nv):
        total = mix[u, 0] * chars[0]
        for v in range(1, nv):
            total = total + mix[u, v] * chars[v]
        new = state[u] + total
        out[u] = new
        turned = jnp.transpose(new)
        lo_i[u : u + 1, :] = turned[ni - 1 : ni, :]
        hi_i[u : u + 1, :] = turned[0:1, :]


def _call(kernel, n_in, smem_at, outs, scratch):
    specs = [_smem() if k in smem_at else _vmem() for k in range(n_in)]
    return pl.pallas_call(
        kernel,
        out_shape=outs,
        in_specs=specs,
        out_specs=tuple(_vmem() for _ in outs) if isinstance(outs, tuple) else _vmem(),
        scratch_shapes=scratch,
    )


def local(
    adjoint,
    source,
    diagonal,
    weight_i,
    weight_j,
    weight_k,
    eigvec,
    eigvec_inv,
    block_inv_i,
    block_inv_j,
    band_i,
    band_j,
):
    nv = adjoint.shape[0]
    nj, ni = adjoint.shape[2], adjoint.shape[3]
    width = block_inv_i.shape[-1]
    state = adjoint.reshape(nv, nj, ni)
    src = source.reshape(nv, nj, ni)
    diag = diagonal.reshape(nv, nj, ni)
    wi = weight_i.reshape(1, nj, ni)
    wj = weight_j.reshape(1, nj, ni)
    wk = weight_k.reshape(1, nj, ni)

    first_i, last_i = inflow_terms(block_inv_i, band_i)
    first_j, last_j = inflow_terms(block_inv_j, band_j)

    blk = jax.ShapeDtypeStruct((nv, nj, ni), jnp.float32)
    ends_i = jax.ShapeDtypeStruct((lax.axis_size("ia"), 16, nj), jnp.float32)
    ends_j = jax.ShapeDtypeStruct((lax.axis_size("ja"), 32, ni), jnp.float32)
    face = jax.ShapeDtypeStruct((nv, ni), jnp.float32)
    scratch = [pltpu.VMEM((nv, nj, ni), jnp.float32)]
    res_call = _call(residual_kernel, 14, (12,), (blk, blk, ends_i), scratch)
    across_call = _call(across_i_kernel, 9, (0, 3, 8), (blk, ends_j), [])
    update_call = _call(update_kernel, 8, (0, 4, 7), (blk, face, face, face, face), scratch)
    dinv_i_t = jnp.swapaxes(block_inv_i, 1, 2)
    step_i = carry_step(first_i, last_i).reshape(-1)
    step_j = carry_step(first_j, last_j).reshape(-1)
    me_i = lax.axis_index("ia").astype(jnp.int32).reshape(1)
    me_j = lax.axis_index("ja").astype(jnp.int32).reshape(1)

    residual = src
    faces = (state[:, :, ni - 1], state[:, :, 0], state[:, nj - 1, :], state[:, 0, :])
    for step in range(ITERS):
        lo_i = shifted(faces[0], "ia", 1)
        hi_i = shifted(faces[1], "ia", -1)
        if step == 0:
            lo_j = shifted(faces[2], "ja", 1)
            hi_j = shifted(faces[3], "ja", -1)
        else:
            lo_j, hi_j = faces[2], faces[3]
        lo_k = shifted(state, "ka", 1)
        hi_k = shifted(state, "ka", -1)
        residual, plain_i, ends_i = res_call(
            state, src, diag, wi[0], wj[0], wk[0], lo_i, hi_i, lo_j, hi_j, lo_k, hi_k, eigvec_inv, dinv_i_t
        )
        gathered_i = gather_ends(ends_i, "ia")
        plain_j, ends_j = across_call(
            me_i, plain_i, gathered_i, step_i, first_i, last_i, block_inv_j, state, eigvec
        )
        gathered_j = gather_ends(ends_j, "ja")
        state, *faces = update_call(me_j, state, plain_j, gathered_j, step_j, first_j, last_j, eigvec)
    return (state.reshape(adjoint.shape), residual.reshape(adjoint.shape))


def solution(mesh):
    return jax.shard_map(
        local,
        mesh=mesh,
        in_specs=(
            P(None, "ka", "ja", "ia"),
            P(None, "ka", "ja", "ia"),
            P(None, "ka", "ja", "ia"),
            P("ka", "ja", "ia"),
            P("ka", "ja", "ia"),
            P("ka", "ja", "ia"),
            P(),
            P(),
            P(),
            P(),
            P(),
            P(),
        ),
        out_specs=(P(None, "ka", "ja", "ia"), P(None, "ka", "ja", "ia")),
        check_vma=False,
    )
```

```python
import jax
import jax.numpy as jnp
from jax import lax
from jax.experimental import pallas as pl
from jax.experimental.pallas import tpu as pltpu
from jax.sharding import PartitionSpec as P

ITERS = 2
HI = lax.Precision.HIGHEST


def shifted(value, axis, by):
    length = lax.axis_size(axis)
    pairs = [(i, i + by) for i in range(length) if 0 <= i + by < length]
    return lax.ppermute(value, axis, pairs)


def inflow_terms(dinv, band):
    coef_one = band[:, 0][:, None]
    coef_two = band[:, 1][:, None]
    resp_last = -(coef_one * dinv[:, :, 0] + coef_two * dinv[:, :, 1])
    resp_first = -coef_two * dinv[:, :, 0]
    return resp_first, resp_last


def carry_step(resp_first, resp_last):
    width = resp_first.shape[-1]
    top = jnp.stack([resp_first[:, width - 2], resp_last[:, width - 2]])
    bottom = jnp.stack([resp_first[:, width - 1], resp_last[:, width - 1]])
    return jnp.stack([top, bottom])


def gather_ends(copies, axis):
    return lax.all_to_all(copies, axis, 0, 0, tiled=True)


def _vmem():
    return pl.BlockSpec(memory_space=pltpu.VMEM)


def _smem():
    return pl.BlockSpec(memory_space=pltpu.SMEM)


def _mm(a, b):
    return jnp.dot(a, b, precision=HI, preferred_element_type=jnp.float32)


def _stack_rows(rows, height):
    row = lax.broadcasted_iota(jnp.int32, (height, rows[0].shape[-1]), 0)
    tile = jnp.zeros((height, rows[0].shape[-1]), jnp.float32)
    for k, r in enumerate(rows):
        tile = jnp.where(row == k, r, tile)
    return tile


def _emit_copies(ends_out, first_rows, last_rows):
    top = _stack_rows(first_rows, 8)
    bottom = _stack_rows(last_rows, 8)
    for c in range(ends_out.shape[0]):
        ends_out[c, 0:8, :] = top
        ends_out[c, 8:16, :] = bottom


def _coef(step, a, d, nv, n):
    row = lax.broadcasted_iota(jnp.int32, (8, n), 0)
    tile = jnp.zeros((8, n), jnp.float32)
    for v in range(nv):
        tile = jnp.where(row == v, step[(a * 2 + d) * nv + v], tile)
    return tile


def _column(vec, shape):
    return jnp.transpose(jnp.broadcast_to(vec, (shape[1], shape[0])))


def residual_kernel(state, src, diag, wi, wj, wk, lo_i, hi_i, lo_j, hi_j, lo_k, hi_k, mix, dinv_t,
                    res_out, plain_out, ends_out, chars):
    nv, nj, ni = state.shape
    lane = lax.broadcasted_iota(jnp.int32, (nj, ni), 1)
    row = lax.broadcasted_iota(jnp.int32, (nj, ni), 0)
    for v in range(nv):
        x = state[v]
        right_i = jnp.where(lane == ni - 1, _column(hi_i[v : v + 1, :], (nj, ni)), pltpu.roll(x, ni - 1, 1))
        left_i = jnp.where(lane == 0, _column(lo_i[v : v + 1, :], (nj, ni)), pltpu.roll(x, 1, 1))
        up_j = jnp.where(row == nj - 1, hi_j[v : v + 1, :], pltpu.roll(x, nj - 1, 0))
        down_j = jnp.where(row == 0, lo_j[v : v + 1, :], pltpu.roll(x, 1, 0))
        res_out[v] = (
            src[v]
            - diag[v] * x
            + wi[...] * (right_i + left_i)
            + wj[...] * (up_j + down_j)
            + wk[...] * (hi_k[v] + lo_k[v])
        )
    for u in range(nv):
        acc = mix[u, 0] * res_out[0]
        for v in range(1, nv):
            acc = acc + mix[u, v] * res_out[v]
        chars[u] = acc
    first_rows, last_rows = [], []
    for u in range(nv):
        plain = _mm(chars[u], dinv_t[u])
        plain_out[u] = plain
        turned = jnp.transpose(plain)
        first_rows.append(turned[ni - 2 : ni - 1, :])
        last_rows.append(turned[ni - 1 : ni, :])
    _emit_copies(ends_out, first_rows, last_rows)


def _inbound(gathered, step, me, nv):
    n = gathered.shape[-1]
    zero = jnp.zeros((8, n), jnp.float32)
    m00, m01 = _coef(step, 0, 0, nv, n), _coef(step, 0, 1, nv, n)
    m10, m11 = _coef(step, 1, 0, nv, n), _coef(step, 1, 1, nv, n)

    def body(c, carry):
        e0, e1 = carry
        n0 = m00 * e0 + m01 * e1 + gathered[c, 0:8, :]
        n1 = m10 * e0 + m11 * e1 + gathered[c, 8:16, :]
        return n0, n1

    return lax.fori_loop(0, me, body, (zero, zero))


def _around(gathered, step, me, nv):
    count, n = gathered.shape[0], gathered.shape[-1]
    zero = jnp.zeros((8, n), jnp.float32)
    m00, m01 = _coef(step, 0, 0, nv, n), _coef(step, 0, 1, nv, n)
    m10, m11 = _coef(step, 1, 0, nv, n), _coef(step, 1, 1, nv, n)

    def advance(e0, e1, c):
        return m00 * e0 + m01 * e1 + gathered[c, 0:8, :], m10 * e0 + m11 * e1 + gathered[c, 8:16, :]

    prev0, prev1 = lax.fori_loop(0, jnp.maximum(me - 1, 0), lambda c, e: advance(e[0], e[1], c), (zero, zero))
    stepped = advance(prev0, prev1, jnp.maximum(me - 1, 0))
    mine0 = jnp.where(me >= 1, stepped[0], zero)
    mine1 = jnp.where(me >= 1, stepped[1], zero)
    next0, next1 = advance(mine0, mine1, me)
    return (prev0, prev1), (mine0, mine1), (next0, next1)


def across_i_kernel(me, plain, gathered, step, first, last, dinv, state, back, out, ends_out):
    nv, nj, ni = plain.shape
    in_first, in_last = _inbound(gathered, step, me[0], nv)
    first_rows, last_rows = [], []
    for v in range(nv):
        fixed = (
            plain[v]
            + _column(in_first[v : v + 1, :], (nj, ni)) * first[v : v + 1, :]
            + _column(in_last[v : v + 1, :], (nj, ni)) * last[v : v + 1, :]
        )
        solved = _mm(dinv[v], fixed)
        out[v] = solved
        first_rows.append(solved[nj - 2 : nj - 1, :])
        last_rows.append(solved[nj - 1 : nj, :])
    _emit_copies(ends_out, first_rows, last_rows)
    if ends_out.shape[1] == 16:
        return
    bottom_rows, top_rows = [], []
    for u in range(nv):
        low = state[u, 0:1, :]
        high = state[u, nj - 1 : nj, :]
        for v in range(nv):
            low = low + back[u, v] * out[v, 0:1, :]
            high = high + back[u, v] * out[v, nj - 1 : nj, :]
        bottom_rows.append(low)
        top_rows.append(high)
    low_tile = _stack_rows(bottom_rows, 8)
    high_tile = _stack_rows(top_rows, 8)
    for c in range(ends_out.shape[0]):
        ends_out[c, 16:24, :] = low_tile
        ends_out[c, 24:32, :] = high_tile


def final_update_kernel(me, state, plain, gathered, step, first, last, mix, out, chars):
    nv, nj, ni = plain.shape
    in_first, in_last = _inbound(gathered, step, me[0], nv)
    for v in range(nv):
        chars[v] = (
            plain[v]
            + in_first[v : v + 1, :] * _column(first[v : v + 1, :], (nj, ni))
            + in_last[v : v + 1, :] * _column(last[v : v + 1, :], (nj, ni))
        )
    for u in range(nv):
        total = mix[u, 0] * chars[0]
        for v in range(1, nv):
            total = total + mix[u, v] * chars[v]
        out[u] = state[u] + total


def update_kernel(me, state, plain, gathered, step, first, last, mix, out, lo_i, hi_i, lo_j, hi_j, chars):
    nv, nj, ni = plain.shape
    count = gathered.shape[0]
    here = me[0]
    prev, (in_first, in_last), nxt = _around(gathered, step, here, nv)
    below = gathered[jnp.maximum(here - 1, 0), 24:32, :]
    above = gathered[jnp.minimum(here + 1, count - 1), 16:24, :]
    for u in range(nv):
        low = below[u : u + 1, :]
        high = above[u : u + 1, :]
        for v in range(nv):
            low = low + mix[u, v] * (
                prev[0][v : v + 1, :] * first[v : v + 1, nj - 1 : nj] + prev[1][v : v + 1, :] * last[v : v + 1, nj - 1 : nj]
            )
            high = high + mix[u, v] * (
                nxt[0][v : v + 1, :] * first[v : v + 1, 0:1] + nxt[1][v : v + 1, :] * last[v : v + 1, 0:1]
            )
        lo_j[u : u + 1, :] = jnp.where(here >= 1, low, 0.0)
        hi_j[u : u + 1, :] = jnp.where(here + 1 < count, high, 0.0)
    for v in range(nv):
        chars[v] = (
            plain[v]
            + in_first[v : v + 1, :] * _column(first[v : v + 1, :], (nj, ni))
            + in_last[v : v + 1, :] * _column(last[v : v + 1, :], (nj, ni))
        )
    for u in range(nv):
        total = mix[u, 0] * chars[0]
        for v in range(1, nv):
            total = total + mix[u, v] * chars[v]
        new = state[u] + total
        out[u] = new
        turned = jnp.transpose(new)
        lo_i[u : u + 1, :] = turned[ni - 1 : ni, :]
        hi_i[u : u + 1, :] = turned[0:1, :]


def _call(kernel, n_in, smem_at, outs, scratch):
    specs = [_smem() if k in smem_at else _vmem() for k in range(n_in)]
    return pl.pallas_call(
        kernel,
        out_shape=outs,
        in_specs=specs,
        out_specs=tuple(_vmem() for _ in outs) if isinstance(outs, tuple) else _vmem(),
        scratch_shapes=scratch,
    )


def local(
    adjoint,
    source,
    diagonal,
    weight_i,
    weight_j,
    weight_k,
    eigvec,
    eigvec_inv,
    block_inv_i,
    block_inv_j,
    band_i,
    band_j,
):
    nv = adjoint.shape[0]
    nj, ni = adjoint.shape[2], adjoint.shape[3]
    width = block_inv_i.shape[-1]
    state = adjoint.reshape(nv, nj, ni)
    src = source.reshape(nv, nj, ni)
    diag = diagonal.reshape(nv, nj, ni)
    wi = weight_i.reshape(1, nj, ni)
    wj = weight_j.reshape(1, nj, ni)
    wk = weight_k.reshape(1, nj, ni)

    first_i, last_i = inflow_terms(block_inv_i, band_i)
    first_j, last_j = inflow_terms(block_inv_j, band_j)

    blk = jax.ShapeDtypeStruct((nv, nj, ni), jnp.float32)
    ends_i = jax.ShapeDtypeStruct((lax.axis_size("ia"), 16, nj), jnp.float32)
    ends_j = jax.ShapeDtypeStruct((lax.axis_size("ja"), 32, ni), jnp.float32)
    face = jax.ShapeDtypeStruct((nv, ni), jnp.float32)
    scratch = [pltpu.VMEM((nv, nj, ni), jnp.float32)]
    res_call = _call(residual_kernel, 14, (12,), (blk, blk, ends_i), scratch)
    across_call = _call(across_i_kernel, 9, (0, 3, 8), (blk, ends_j), [])
    ends_j_last = jax.ShapeDtypeStruct((lax.axis_size("ja"), 16, ni), jnp.float32)
    across_last_call = _call(across_i_kernel, 9, (0, 3, 8), (blk, ends_j_last), [])
    update_call = _call(update_kernel, 8, (0, 4, 7), (blk, face, face, face, face), scratch)
    final_call = _call(final_update_kernel, 8, (0, 4, 7), blk, scratch)
    dinv_i_t = jnp.swapaxes(block_inv_i, 1, 2)
    step_i = carry_step(first_i, last_i).reshape(-1)
    step_j = carry_step(first_j, last_j).reshape(-1)
    me_i = lax.axis_index("ia").astype(jnp.int32).reshape(1)
    me_j = lax.axis_index("ja").astype(jnp.int32).reshape(1)

    residual = src
    faces = (state[:, :, ni - 1], state[:, :, 0], state[:, nj - 1, :], state[:, 0, :])
    for step in range(ITERS):
        lo_i = shifted(faces[0], "ia", 1)
        hi_i = shifted(faces[1], "ia", -1)
        if step == 0:
            lo_j = shifted(faces[2], "ja", 1)
            hi_j = shifted(faces[3], "ja", -1)
        else:
            lo_j, hi_j = faces[2], faces[3]
        lo_k = shifted(state, "ka", 1)
        hi_k = shifted(state, "ka", -1)
        residual, plain_i, ends_i = res_call(
            state, src, diag, wi[0], wj[0], wk[0], lo_i, hi_i, lo_j, hi_j, lo_k, hi_k, eigvec_inv, dinv_i_t
        )
        gathered_i = gather_ends(ends_i, "ia")
        last_step = step + 1 == ITERS
        plain_j, ends_j = (across_last_call if last_step else across_call)(
            me_i, plain_i, gathered_i, step_i, first_i, last_i, block_inv_j, state, eigvec
        )
        gathered_j = gather_ends(ends_j, "ja")
        if last_step:
            state = final_call(me_j, state, plain_j, gathered_j, step_j, first_j, last_j, eigvec)
        else:
            state, *faces = update_call(me_j, state, plain_j, gathered_j, step_j, first_j, last_j, eigvec)
    return (state.reshape(adjoint.shape), residual.reshape(adjoint.shape))


def solution(mesh):
    return jax.shard_map(
        local,
        mesh=mesh,
        in_specs=(
            P(None, "ka", "ja", "ia"),
            P(None, "ka", "ja", "ia"),
            P(None, "ka", "ja", "ia"),
            P("ka", "ja", "ia"),
            P("ka", "ja", "ia"),
            P("ka", "ja", "ia"),
            P(),
            P(),
            P(),
            P(),
            P(),
            P(),
        ),
        out_specs=(P(None, "ka", "ja", "ia"), P(None, "ka", "ja", "ia")),
        check_vma=False,
    )
```

```python
import jax
import jax.numpy as jnp
from jax import lax
from jax.experimental import pallas as pl
from jax.experimental.pallas import tpu as pltpu
from jax.sharding import PartitionSpec as P

ITERS = 2
HI = lax.Precision.HIGHEST


def shifted(value, axis, by):
    length = lax.axis_size(axis)
    pairs = [(i, i + by) for i in range(length) if 0 <= i + by < length]
    return lax.ppermute(value, axis, pairs)


def inflow_terms(dinv, band):
    coef_one = band[:, 0][:, None]
    coef_two = band[:, 1][:, None]
    resp_last = -(coef_one * dinv[:, :, 0] + coef_two * dinv[:, :, 1])
    resp_first = -coef_two * dinv[:, :, 0]
    return resp_first, resp_last


def carry_step(resp_first, resp_last):
    width = resp_first.shape[-1]
    top = jnp.stack([resp_first[:, width - 2], resp_last[:, width - 2]])
    bottom = jnp.stack([resp_first[:, width - 1], resp_last[:, width - 1]])
    return jnp.stack([top, bottom])


def gather_ends(copies, axis):
    return lax.all_to_all(copies, axis, 0, 0, tiled=True)


def _vmem():
    return pl.BlockSpec(memory_space=pltpu.VMEM)


def _smem():
    return pl.BlockSpec(memory_space=pltpu.SMEM)


def _mm(a, b):
    return jnp.dot(a, b, precision=HI, preferred_element_type=jnp.float32)


def _stack_rows(rows, height):
    row = lax.broadcasted_iota(jnp.int32, (height, rows[0].shape[-1]), 0)
    tile = jnp.zeros((height, rows[0].shape[-1]), jnp.float32)
    for k, r in enumerate(rows):
        tile = jnp.where(row == k, r, tile)
    return tile


def _emit_copies(ends_out, first_rows, last_rows):
    top = _stack_rows(first_rows, 8)
    bottom = _stack_rows(last_rows, 8)
    for c in range(ends_out.shape[0]):
        ends_out[c, 0:8, :] = top
        ends_out[c, 8:16, :] = bottom


def _coef(step, a, d, nv, n):
    row = lax.broadcasted_iota(jnp.int32, (8, n), 0)
    tile = jnp.zeros((8, n), jnp.float32)
    for v in range(nv):
        tile = jnp.where(row == v, step[(a * 2 + d) * nv + v], tile)
    return tile


def _column(vec, shape):
    return jnp.transpose(jnp.broadcast_to(vec, (shape[1], shape[0])))


def residual_kernel(state, src, diag, wi, wj, wk, lo_i, hi_i, lo_j, hi_j, lo_k, hi_k, mix, dinv_t,
                    res_out, plain_out, ends_out, chars):
    nv, nj, ni = state.shape
    lane = lax.broadcasted_iota(jnp.int32, (nj, ni), 1)
    row = lax.broadcasted_iota(jnp.int32, (nj, ni), 0)
    for v in range(nv):
        x = state[v]
        right_i = jnp.where(lane == ni - 1, _column(hi_i[v : v + 1, :], (nj, ni)), pltpu.roll(x, ni - 1, 1))
        left_i = jnp.where(lane == 0, _column(lo_i[v : v + 1, :], (nj, ni)), pltpu.roll(x, 1, 1))
        up_j = jnp.where(row == nj - 1, hi_j[v : v + 1, :], pltpu.roll(x, nj - 1, 0))
        down_j = jnp.where(row == 0, lo_j[v : v + 1, :], pltpu.roll(x, 1, 0))
        res_out[v] = (
            src[v]
            - diag[v] * x
            + wi[...] * (right_i + left_i)
            + wj[...] * (up_j + down_j)
            + wk[...] * (hi_k[v] + lo_k[v])
        )
    for u in range(nv):
        acc = mix[u, 0] * res_out[0]
        for v in range(1, nv):
            acc = acc + mix[u, v] * res_out[v]
        chars[u] = acc
    first_rows, last_rows = [], []
    for u in range(nv):
        plain = _mm(chars[u], jnp.transpose(dinv_t[u]))
        plain_out[u] = plain
        turned = jnp.transpose(plain)
        first_rows.append(turned[ni - 2 : ni - 1, :])
        last_rows.append(turned[ni - 1 : ni, :])
    _emit_copies(ends_out, first_rows, last_rows)


def _inbound(gathered, step, me, nv):
    n = gathered.shape[-1]
    zero = jnp.zeros((8, n), jnp.float32)
    m00, m01 = _coef(step, 0, 0, nv, n), _coef(step, 0, 1, nv, n)
    m10, m11 = _coef(step, 1, 0, nv, n), _coef(step, 1, 1, nv, n)

    def body(c, carry):
        e0, e1 = carry
        n0 = m00 * e0 + m01 * e1 + gathered[c, 0:8, :]
        n1 = m10 * e0 + m11 * e1 + gathered[c, 8:16, :]
        return n0, n1

    return lax.fori_loop(0, me, body, (zero, zero))


def _around(gathered, step, me, nv):
    count, n = gathered.shape[0], gathered.shape[-1]
    zero = jnp.zeros((8, n), jnp.float32)
    m00, m01 = _coef(step, 0, 0, nv, n), _coef(step, 0, 1, nv, n)
    m10, m11 = _coef(step, 1, 0, nv, n), _coef(step, 1, 1, nv, n)

    def advance(e0, e1, c):
        return m00 * e0 + m01 * e1 + gathered[c, 0:8, :], m10 * e0 + m11 * e1 + gathered[c, 8:16, :]

    prev0, prev1 = lax.fori_loop(0, jnp.maximum(me - 1, 0), lambda c, e: advance(e[0], e[1], c), (zero, zero))
    stepped = advance(prev0, prev1, jnp.maximum(me - 1, 0))
    mine0 = jnp.where(me >= 1, stepped[0], zero)
    mine1 = jnp.where(me >= 1, stepped[1], zero)
    next0, next1 = advance(mine0, mine1, me)
    return (prev0, prev1), (mine0, mine1), (next0, next1)


def across_i_kernel(me, plain, gathered, step, first, last, dinv, state, back, out, ends_out):
    nv, nj, ni = plain.shape
    in_first, in_last = _inbound(gathered, step, me[0], nv)
    first_rows, last_rows = [], []
    for v in range(nv):
        fixed = (
            plain[v]
            + _column(in_first[v : v + 1, :], (nj, ni)) * first[v : v + 1, :]
            + _column(in_last[v : v + 1, :], (nj, ni)) * last[v : v + 1, :]
        )
        solved = _mm(dinv[v], fixed)
        out[v] = solved
        first_rows.append(solved[nj - 2 : nj - 1, :])
        last_rows.append(solved[nj - 1 : nj, :])
    _emit_copies(ends_out, first_rows, last_rows)
    if ends_out.shape[1] == 16:
        return
    bottom_rows, top_rows = [], []
    for u in range(nv):
        low = state[u, 0:1, :]
        high = state[u, nj - 1 : nj, :]
        for v in range(nv):
            low = low + back[u, v] * out[v, 0:1, :]
            high = high + back[u, v] * out[v, nj - 1 : nj, :]
        bottom_rows.append(low)
        top_rows.append(high)
    low_tile = _stack_rows(bottom_rows, 8)
    high_tile = _stack_rows(top_rows, 8)
    for c in range(ends_out.shape[0]):
        ends_out[c, 16:24, :] = low_tile
        ends_out[c, 24:32, :] = high_tile


def final_update_kernel(me, state, plain, gathered, step, first, last, mix, out, chars):
    nv, nj, ni = plain.shape
    in_first, in_last = _inbound(gathered, step, me[0], nv)
    for v in range(nv):
        chars[v] = (
            plain[v]
            + in_first[v : v + 1, :] * _column(first[v : v + 1, :], (nj, ni))
            + in_last[v : v + 1, :] * _column(last[v : v + 1, :], (nj, ni))
        )
    for u in range(nv):
        total = mix[u, 0] * chars[0]
        for v in range(1, nv):
            total = total + mix[u, v] * chars[v]
        out[u] = state[u] + total


def update_kernel(me, state, plain, gathered, step, first, last, mix, out, lo_i, hi_i, lo_j, hi_j, chars):
    nv, nj, ni = plain.shape
    count = gathered.shape[0]
    here = me[0]
    prev, (in_first, in_last), nxt = _around(gathered, step, here, nv)
    below = gathered[jnp.maximum(here - 1, 0), 24:32, :]
    above = gathered[jnp.minimum(here + 1, count - 1), 16:24, :]
    for u in range(nv):
        low = below[u : u + 1, :]
        high = above[u : u + 1, :]
        for v in range(nv):
            low = low + mix[u, v] * (
                prev[0][v : v + 1, :] * first[v : v + 1, nj - 1 : nj] + prev[1][v : v + 1, :] * last[v : v + 1, nj - 1 : nj]
            )
            high = high + mix[u, v] * (
                nxt[0][v : v + 1, :] * first[v : v + 1, 0:1] + nxt[1][v : v + 1, :] * last[v : v + 1, 0:1]
            )
        lo_j[u : u + 1, :] = jnp.where(here >= 1, low, 0.0)
        hi_j[u : u + 1, :] = jnp.where(here + 1 < count, high, 0.0)
    for v in range(nv):
        chars[v] = (
            plain[v]
            + in_first[v : v + 1, :] * _column(first[v : v + 1, :], (nj, ni))
            + in_last[v : v + 1, :] * _column(last[v : v + 1, :], (nj, ni))
        )
    for u in range(nv):
        total = mix[u, 0] * chars[0]
        for v in range(1, nv):
            total = total + mix[u, v] * chars[v]
        new = state[u] + total
        out[u] = new
        turned = jnp.transpose(new)
        lo_i[u : u + 1, :] = turned[ni - 1 : ni, :]
        hi_i[u : u + 1, :] = turned[0:1, :]


def _call(kernel, n_in, smem_at, outs, scratch):
    specs = [_smem() if k in smem_at else _vmem() for k in range(n_in)]
    return pl.pallas_call(
        kernel,
        out_shape=outs,
        in_specs=specs,
        out_specs=tuple(_vmem() for _ in outs) if isinstance(outs, tuple) else _vmem(),
        scratch_shapes=scratch,
    )


def local(
    adjoint,
    source,
    diagonal,
    weight_i,
    weight_j,
    weight_k,
    eigvec,
    eigvec_inv,
    block_inv_i,
    block_inv_j,
    band_i,
    band_j,
):
    nv = adjoint.shape[0]
    nj, ni = adjoint.shape[2], adjoint.shape[3]
    width = block_inv_i.shape[-1]
    state = adjoint.reshape(nv, nj, ni)
    src = source.reshape(nv, nj, ni)
    diag = diagonal.reshape(nv, nj, ni)
    wi = weight_i.reshape(1, nj, ni)
    wj = weight_j.reshape(1, nj, ni)
    wk = weight_k.reshape(1, nj, ni)

    first_i, last_i = inflow_terms(block_inv_i, band_i)
    first_j, last_j = inflow_terms(block_inv_j, band_j)

    blk = jax.ShapeDtypeStruct((nv, nj, ni), jnp.float32)
    ends_i = jax.ShapeDtypeStruct((lax.axis_size("ia"), 16, nj), jnp.float32)
    ends_j = jax.ShapeDtypeStruct((lax.axis_size("ja"), 32, ni), jnp.float32)
    face = jax.ShapeDtypeStruct((nv, ni), jnp.float32)
    scratch = [pltpu.VMEM((nv, nj, ni), jnp.float32)]
    res_call = _call(residual_kernel, 14, (12,), (blk, blk, ends_i), scratch)
    across_call = _call(across_i_kernel, 9, (0, 3, 8), (blk, ends_j), [])
    ends_j_last = jax.ShapeDtypeStruct((lax.axis_size("ja"), 16, ni), jnp.float32)
    across_last_call = _call(across_i_kernel, 9, (0, 3, 8), (blk, ends_j_last), [])
    update_call = _call(update_kernel, 8, (0, 4, 7), (blk, face, face, face, face), scratch)
    final_call = _call(final_update_kernel, 8, (0, 4, 7), blk, scratch)
    step_i = carry_step(first_i, last_i).reshape(-1)
    step_j = carry_step(first_j, last_j).reshape(-1)
    me_i = lax.axis_index("ia").astype(jnp.int32).reshape(1)
    me_j = lax.axis_index("ja").astype(jnp.int32).reshape(1)

    residual = src
    faces = (state[:, :, ni - 1], state[:, :, 0], state[:, nj - 1, :], state[:, 0, :])
    for step in range(ITERS):
        lo_i = shifted(faces[0], "ia", 1)
        hi_i = shifted(faces[1], "ia", -1)
        if step == 0:
            lo_j = shifted(faces[2], "ja", 1)
            hi_j = shifted(faces[3], "ja", -1)
        else:
            lo_j, hi_j = faces[2], faces[3]
        lo_k = shifted(state, "ka", 1)
        hi_k = shifted(state, "ka", -1)
        residual, plain_i, ends_i = res_call(
            state, src, diag, wi[0], wj[0], wk[0], lo_i, hi_i, lo_j, hi_j, lo_k, hi_k, eigvec_inv, block_inv_i
        )
        gathered_i = gather_ends(ends_i, "ia")
        last_step = step + 1 == ITERS
        plain_j, ends_j = (across_last_call if last_step else across_call)(
            me_i, plain_i, gathered_i, step_i, first_i, last_i, block_inv_j, state, eigvec
        )
        gathered_j = gather_ends(ends_j, "ja")
        if last_step:
            state = final_call(me_j, state, plain_j, gathered_j, step_j, first_j, last_j, eigvec)
        else:
            state, *faces = update_call(me_j, state, plain_j, gathered_j, step_j, first_j, last_j, eigvec)
    return (state.reshape(adjoint.shape), residual.reshape(adjoint.shape))


def solution(mesh):
    return jax.shard_map(
        local,
        mesh=mesh,
        in_specs=(
            P(None, "ka", "ja", "ia"),
            P(None, "ka", "ja", "ia"),
            P(None, "ka", "ja", "ia"),
            P("ka", "ja", "ia"),
            P("ka", "ja", "ia"),
            P("ka", "ja", "ia"),
            P(),
            P(),
            P(),
            P(),
            P(),
            P(),
        ),
        out_specs=(P(None, "ka", "ja", "ia"), P(None, "ka", "ja", "ia")),
        check_vma=False,
    )
```

```python
import jax
import jax.numpy as jnp
from jax import lax
from jax.experimental import pallas as pl
from jax.experimental.pallas import tpu as pltpu
from jax.sharding import PartitionSpec as P

ITERS = 2
HI = lax.Precision.HIGHEST


def shifted(value, axis, by):
    length = lax.axis_size(axis)
    pairs = [(i, i + by) for i in range(length) if 0 <= i + by < length]
    return lax.ppermute(value, axis, pairs)


def inflow_terms(dinv, band):
    coef_one = band[:, 0][:, None]
    coef_two = band[:, 1][:, None]
    resp_last = -(coef_one * dinv[:, :, 0] + coef_two * dinv[:, :, 1])
    resp_first = -coef_two * dinv[:, :, 0]
    return resp_first, resp_last


def carry_step(resp_first, resp_last):
    width = resp_first.shape[-1]
    top = jnp.stack([resp_first[:, width - 2], resp_last[:, width - 2]])
    bottom = jnp.stack([resp_first[:, width - 1], resp_last[:, width - 1]])
    return jnp.stack([top, bottom])


def gather_ends(copies, axis):
    return lax.all_to_all(copies, axis, 0, 0, tiled=True)


def _vmem():
    return pl.BlockSpec(memory_space=pltpu.VMEM)


def _smem():
    return pl.BlockSpec(memory_space=pltpu.SMEM)


def _mm(a, b):
    return jnp.dot(a, b, precision=HI, preferred_element_type=jnp.float32)


def _stack_rows(rows, height):
    row = lax.broadcasted_iota(jnp.int32, (height, rows[0].shape[-1]), 0)
    tile = jnp.zeros((height, rows[0].shape[-1]), jnp.float32)
    for k, r in enumerate(rows):
        tile = jnp.where(row == k, r, tile)
    return tile


def _emit_copies(ends_out, first_rows, last_rows):
    top = _stack_rows(first_rows, 8)
    bottom = _stack_rows(last_rows, 8)
    for c in range(ends_out.shape[0]):
        ends_out[c, 0:8, :] = top
        ends_out[c, 8:16, :] = bottom


def _coef(step, a, d, nv, n):
    row = lax.broadcasted_iota(jnp.int32, (8, n), 0)
    tile = jnp.zeros((8, n), jnp.float32)
    for v in range(nv):
        tile = jnp.where(row == v, step[(a * 2 + d) * nv + v], tile)
    return tile


def _column(vec, shape):
    return jnp.transpose(jnp.broadcast_to(vec, (shape[1], shape[0])))


def residual_kernel(state, src, diag, wi, wj, wk, lo_i, hi_i, lo_j, hi_j, lo_k, hi_k, mix, dinv_t,
                    res_out, plain_out, ends_out, chars):
    nv, nj, ni = state.shape
    lane = lax.broadcasted_iota(jnp.int32, (nj, ni), 1)
    row = lax.broadcasted_iota(jnp.int32, (nj, ni), 0)
    for v in range(nv):
        x = state[v]
        right_i = jnp.where(lane == ni - 1, _column(hi_i[v : v + 1, :], (nj, ni)), pltpu.roll(x, ni - 1, 1))
        left_i = jnp.where(lane == 0, _column(lo_i[v : v + 1, :], (nj, ni)), pltpu.roll(x, 1, 1))
        up_j = jnp.where(row == nj - 1, hi_j[v : v + 1, :], pltpu.roll(x, nj - 1, 0))
        down_j = jnp.where(row == 0, lo_j[v : v + 1, :], pltpu.roll(x, 1, 0))
        res_out[v] = (
            src[v]
            - diag[v] * x
            + wi[...] * (right_i + left_i)
            + wj[...] * (up_j + down_j)
            + wk[...] * (hi_k[v] + lo_k[v])
        )
    for u in range(nv):
        acc = mix[u, 0] * res_out[0]
        for v in range(1, nv):
            acc = acc + mix[u, v] * res_out[v]
        chars[u] = acc
    first_rows, last_rows = [], []
    for u in range(nv):
        plain = _mm(chars[u], dinv_t[u])
        plain_out[u] = plain
        turned = jnp.transpose(plain)
        first_rows.append(turned[ni - 2 : ni - 1, :])
        last_rows.append(turned[ni - 1 : ni, :])
    _emit_copies(ends_out, first_rows, last_rows)


def _inbound(gathered, step, me, nv):
    n = gathered.shape[-1]
    zero = jnp.zeros((8, n), jnp.float32)
    m00, m01 = _coef(step, 0, 0, nv, n), _coef(step, 0, 1, nv, n)
    m10, m11 = _coef(step, 1, 0, nv, n), _coef(step, 1, 1, nv, n)

    def body(c, carry):
        e0, e1 = carry
        n0 = m00 * e0 + m01 * e1 + gathered[c, 0:8, :]
        n1 = m10 * e0 + m11 * e1 + gathered[c, 8:16, :]
        return n0, n1

    return lax.fori_loop(0, me, body, (zero, zero))


def _around(gathered, step, me, nv):
    count, n = gathered.shape[0], gathered.shape[-1]
    zero = jnp.zeros((8, n), jnp.float32)
    m00, m01 = _coef(step, 0, 0, nv, n), _coef(step, 0, 1, nv, n)
    m10, m11 = _coef(step, 1, 0, nv, n), _coef(step, 1, 1, nv, n)

    def advance(e0, e1, c):
        return m00 * e0 + m01 * e1 + gathered[c, 0:8, :], m10 * e0 + m11 * e1 + gathered[c, 8:16, :]

    prev0, prev1 = lax.fori_loop(0, jnp.maximum(me - 1, 0), lambda c, e: advance(e[0], e[1], c), (zero, zero))
    stepped = advance(prev0, prev1, jnp.maximum(me - 1, 0))
    mine0 = jnp.where(me >= 1, stepped[0], zero)
    mine1 = jnp.where(me >= 1, stepped[1], zero)
    next0, next1 = advance(mine0, mine1, me)
    return (prev0, prev1), (mine0, mine1), (next0, next1)


def across_i_kernel(me, plain, gathered, step, first, last, dinv, state, back, out, ends_out):
    nv, nj, ni = plain.shape
    in_first, in_last = _inbound(gathered, step, me[0], nv)
    first_rows, last_rows = [], []
    for v in range(nv):
        fixed = (
            plain[v]
            + _column(in_first[v : v + 1, :], (nj, ni)) * first[v : v + 1, :]
            + _column(in_last[v : v + 1, :], (nj, ni)) * last[v : v + 1, :]
        )
        solved = _mm(dinv[v], fixed)
        out[v] = solved
        first_rows.append(solved[nj - 2 : nj - 1, :])
        last_rows.append(solved[nj - 1 : nj, :])
    _emit_copies(ends_out, first_rows, last_rows)
    if ends_out.shape[1] == 16:
        return
    bottom_rows, top_rows = [], []
    for u in range(nv):
        low = state[u, 0:1, :]
        high = state[u, nj - 1 : nj, :]
        for v in range(nv):
            low = low + back[u, v] * out[v, 0:1, :]
            high = high + back[u, v] * out[v, nj - 1 : nj, :]
        bottom_rows.append(low)
        top_rows.append(high)
    low_tile = _stack_rows(bottom_rows, 8)
    high_tile = _stack_rows(top_rows, 8)
    for c in range(ends_out.shape[0]):
        ends_out[c, 16:24, :] = low_tile
        ends_out[c, 24:32, :] = high_tile


def final_update_kernel(me, state, plain, gathered, step, first, last, mix, out, chars):
    nv, nj, ni = plain.shape
    in_first, in_last = _inbound(gathered, step, me[0], nv)
    for v in range(nv):
        chars[v] = (
            plain[v]
            + in_first[v : v + 1, :] * _column(first[v : v + 1, :], (nj, ni))
            + in_last[v : v + 1, :] * _column(last[v : v + 1, :], (nj, ni))
        )
    for u in range(nv):
        total = mix[u, 0] * chars[0]
        for v in range(1, nv):
            total = total + mix[u, v] * chars[v]
        out[u] = state[u] + total


def update_kernel(me, state, plain, gathered, step, first, last, mix, out, lo_i, hi_i, lo_j, hi_j, chars):
    nv, nj, ni = plain.shape
    count = gathered.shape[0]
    here = me[0]
    prev, (in_first, in_last), nxt = _around(gathered, step, here, nv)
    below = gathered[jnp.maximum(here - 1, 0), 24:32, :]
    above = gathered[jnp.minimum(here + 1, count - 1), 16:24, :]
    for u in range(nv):
        low = below[u : u + 1, :]
        high = above[u : u + 1, :]
        for v in range(nv):
            low = low + mix[u, v] * (
                prev[0][v : v + 1, :] * first[v : v + 1, nj - 1 : nj] + prev[1][v : v + 1, :] * last[v : v + 1, nj - 1 : nj]
            )
            high = high + mix[u, v] * (
                nxt[0][v : v + 1, :] * first[v : v + 1, 0:1] + nxt[1][v : v + 1, :] * last[v : v + 1, 0:1]
            )
        lo_j[u : u + 1, :] = jnp.where(here >= 1, low, 0.0)
        hi_j[u : u + 1, :] = jnp.where(here + 1 < count, high, 0.0)
    for v in range(nv):
        chars[v] = (
            plain[v]
            + in_first[v : v + 1, :] * _column(first[v : v + 1, :], (nj, ni))
            + in_last[v : v + 1, :] * _column(last[v : v + 1, :], (nj, ni))
        )
    for u in range(nv):
        total = mix[u, 0] * chars[0]
        for v in range(1, nv):
            total = total + mix[u, v] * chars[v]
        new = state[u] + total
        out[u] = new
        turned = jnp.transpose(new)
        lo_i[u : u + 1, :] = turned[ni - 1 : ni, :]
        hi_i[u : u + 1, :] = turned[0:1, :]


def faces_kernel(state, lo_i, hi_i, lo_j, hi_j):
    nv, nj, ni = state.shape
    for u in range(nv):
        x = state[u]
        turned = jnp.transpose(x)
        lo_i[u : u + 1, :] = turned[ni - 1 : ni, :]
        hi_i[u : u + 1, :] = turned[0:1, :]
        lo_j[u : u + 1, :] = x[nj - 1 : nj, :]
        hi_j[u : u + 1, :] = x[0:1, :]


def _call(kernel, n_in, smem_at, outs, scratch):
    specs = [_smem() if k in smem_at else _vmem() for k in range(n_in)]
    return pl.pallas_call(
        kernel,
        out_shape=outs,
        in_specs=specs,
        out_specs=tuple(_vmem() for _ in outs) if isinstance(outs, tuple) else _vmem(),
        scratch_shapes=scratch,
    )


def local(
    adjoint,
    source,
    diagonal,
    weight_i,
    weight_j,
    weight_k,
    eigvec,
    eigvec_inv,
    block_inv_i,
    block_inv_j,
    band_i,
    band_j,
):
    nv = adjoint.shape[0]
    nj, ni = adjoint.shape[2], adjoint.shape[3]
    width = block_inv_i.shape[-1]
    state = adjoint.reshape(nv, nj, ni)
    src = source.reshape(nv, nj, ni)
    diag = diagonal.reshape(nv, nj, ni)
    wi = weight_i.reshape(1, nj, ni)
    wj = weight_j.reshape(1, nj, ni)
    wk = weight_k.reshape(1, nj, ni)

    first_i, last_i = inflow_terms(block_inv_i, band_i)
    first_j, last_j = inflow_terms(block_inv_j, band_j)

    blk = jax.ShapeDtypeStruct((nv, nj, ni), jnp.float32)
    ends_i = jax.ShapeDtypeStruct((lax.axis_size("ia"), 16, nj), jnp.float32)
    ends_j = jax.ShapeDtypeStruct((lax.axis_size("ja"), 32, ni), jnp.float32)
    face = jax.ShapeDtypeStruct((nv, ni), jnp.float32)
    scratch = [pltpu.VMEM((nv, nj, ni), jnp.float32)]
    res_call = _call(residual_kernel, 14, (12,), (blk, blk, ends_i), scratch)
    across_call = _call(across_i_kernel, 9, (0, 3, 8), (blk, ends_j), [])
    ends_j_last = jax.ShapeDtypeStruct((lax.axis_size("ja"), 16, ni), jnp.float32)
    across_last_call = _call(across_i_kernel, 9, (0, 3, 8), (blk, ends_j_last), [])
    update_call = _call(update_kernel, 8, (0, 4, 7), (blk, face, face, face, face), scratch)
    final_call = _call(final_update_kernel, 8, (0, 4, 7), blk, scratch)
    dinv_i_t = jnp.swapaxes(block_inv_i, 1, 2)
    step_i = carry_step(first_i, last_i).reshape(-1)
    step_j = carry_step(first_j, last_j).reshape(-1)
    me_i = lax.axis_index("ia").astype(jnp.int32).reshape(1)
    me_j = lax.axis_index("ja").astype(jnp.int32).reshape(1)

    residual = src
    faces = _call(faces_kernel, 1, (), (face, face, face, face), [])(state)
    for step in range(ITERS):
        lo_i = shifted(faces[0], "ia", 1)
        hi_i = shifted(faces[1], "ia", -1)
        if step == 0:
            lo_j = shifted(faces[2], "ja", 1)
            hi_j = shifted(faces[3], "ja", -1)
        else:
            lo_j, hi_j = faces[2], faces[3]
        lo_k = shifted(state, "ka", 1)
        hi_k = shifted(state, "ka", -1)
        residual, plain_i, ends_i = res_call(
            state, src, diag, wi[0], wj[0], wk[0], lo_i, hi_i, lo_j, hi_j, lo_k, hi_k, eigvec_inv, dinv_i_t
        )
        gathered_i = gather_ends(ends_i, "ia")
        last_step = step + 1 == ITERS
        plain_j, ends_j = (across_last_call if last_step else across_call)(
            me_i, plain_i, gathered_i, step_i, first_i, last_i, block_inv_j, state, eigvec
        )
        gathered_j = gather_ends(ends_j, "ja")
        if last_step:
            state = final_call(me_j, state, plain_j, gathered_j, step_j, first_j, last_j, eigvec)
        else:
            state, *faces = update_call(me_j, state, plain_j, gathered_j, step_j, first_j, last_j, eigvec)
    return (state.reshape(adjoint.shape), residual.reshape(adjoint.shape))


def solution(mesh):
    return jax.shard_map(
        local,
        mesh=mesh,
        in_specs=(
            P(None, "ka", "ja", "ia"),
            P(None, "ka", "ja", "ia"),
            P(None, "ka", "ja", "ia"),
            P("ka", "ja", "ia"),
            P("ka", "ja", "ia"),
            P("ka", "ja", "ia"),
            P(),
            P(),
            P(),
            P(),
            P(),
            P(),
        ),
        out_specs=(P(None, "ka", "ja", "ia"), P(None, "ka", "ja", "ia")),
        check_vma=False,
    )
```
